256 devices in a mesh: section: 4 (over x), dp: 4 (over y), chan: 16 (over z, core).
Axes of the slice: x: 4, y: 4, z: 8, core: 2. Of those that a mesh axis runs over, the one named last changes fastest.
Arguments:
- feats: bfloat16 [8, 32, 128, 2048], P('dp', None, None, 'chan'), may hold values from -6 to 6
- offsets: int32 [8], P('dp'), may hold values from 0 to 127
- widths: int32 [8], P('dp'), may hold values from 32 to 64
- labels: int32 [8, 32, 128], P('dp'), may hold values from 0 to 19
- dw_kernel: bfloat16 [4, 9, 2048], P('section', None, 'chan'), may hold values from -2 to 2
- pw_weight: bfloat16 [4, 2048, 256], P('section', 'chan'), may hold values from -0.125 to 0.125
- pw_bias: float32 [4, 256], P('section', 'chan'), may hold values from -3 to 3
- proj: bfloat16 [4, 256, 256], P('section', 'chan'), may hold values from -0.1875 to 0.1875
- proj_bias: float32 [256], P('chan'), may hold values from -3 to 3
- upstream: bfloat16 [256, 8, 32, 128], P('chan', 'dp'), may hold values from -6 to 6
Outputs:
- aspp_out: bfloat16 [256, 8, 32, 128], P('chan', 'dp')
- input_grad: bfloat16 [8, 32, 128, 2048], P('dp', 'section', None, 'chan')
- grad_dw: float32 [4, 9, 2048], P('section', None, 'chan')
- grad_pw: float32 [4, 2048, 256], P('section', 'chan')
- grad_pw_bias: float32 [4, 256], P('section', 'chan')
- grad_proj: float32 [4, 256, 256], P('section', 'chan')
- grad_proj_bias: float32 [256], P('chan')
The draws below stay inside these ranges and needn't reach their ends.
All inputs are finite; a program needn't handle non-finite values.
Results may differ from the reference program's by a relative error of at most 0.008.
Values may be sent and summed in bfloat16 or wider, within the bound.
No kernel may reach another device: no remote copies, remote signals or barrier semaphores. Data moves between devices by JAX's collectives and lax.ppermute only.
A program may use at most 128 MiB of HBM per device.

```python
import math
import jax
import jax.numpy as jnp
from jax import lax

C = 2048
BR = 256
FW = 128
FH = 32
RATE = 6
FRAMES = 8
N_SECTION = 4


def with_ends(result, key, least, top_value):
    index_at = [jax.random.randint(jax.random.fold_in(key, axis), (), 0, length) for axis, length in enumerate(result.shape)]
    longest = result.shape.index(max(result.shape))
    neighbour = index_at[:longest] + [(index_at[longest] + 1) % result.shape[longest]] + index_at[longest + 1:]
    return result.at[tuple(index_at)].set(least).at[tuple(neighbour)].set(top_value)


def block_scale(rng, extent, cuts, smallest, high):
    level = 1.0
    for axis_at, parts in cuts:
        draws = jax.random.uniform(jax.random.fold_in(jax.random.fold_in(rng, 6), axis_at), (parts,), jnp.float32, smallest / len(cuts), high / len(cuts))
        level = level * jnp.repeat(jnp.exp(draws), extent[axis_at] // parts).reshape((-1,) + (1,) * (len(extent) - 1 - axis_at))
    return level


def gaussian(key, extent, scale, limit, shards=(), kind=jnp.bfloat16):
    array = jax.random.normal(key, extent, jnp.float32) * scale
    if len(shards) > 0:
        array = block_scale(key, extent, shards, -0.22, 0.18) * array
    return jnp.clip(array, min=-limit, max=limit).astype(kind)


def setup_inputs(seed: int = 0) -> dict:
    key_of = jax.random.split(jax.random.key(seed), 11)
    return {
        "feats": gaussian(key_of[0], (FRAMES, FH, FW, C), 1.0, 6.0, ((0, 4), (3, 16))),
        "offsets": with_ends(jax.random.randint(key_of[1], (FRAMES,), 0, FW), jax.random.fold_in(key_of[1], 1), 0, FW - 1).astype(jnp.int32),
        "widths": with_ends(jax.random.randint(key_of[2], (FRAMES,), FW // 4, FW // 2 + 1), jax.random.fold_in(key_of[2], 1), FW // 4, (FW // 2 + 1) - 1).astype(jnp.int32),
        "labels": with_ends(jax.random.randint(key_of[3], (FRAMES, FH, FW), 0, 20), jax.random.fold_in(key_of[3], 1), 0, 19).astype(jnp.int32),
        "dw_kernel": gaussian(key_of[4], (N_SECTION, 9, C), 9 ** -0.5, 2.0, ((0, 4), (2, 16))),
        "pw_weight": gaussian(key_of[5], (N_SECTION, C, BR), C ** -0.5, 0.125, ((0, 4), (1, 16))),
        "pw_bias": gaussian(key_of[6], (N_SECTION, BR), 0.5, 3.0, ((0, 4), (1, 16)), jnp.float32),
        "proj": gaussian(key_of[7], (N_SECTION, BR, BR), (4 * BR) ** -0.5, 0.1875, ((0, 4), (1, 16))),
        "proj_bias": gaussian(key_of[8], (BR,), 0.5, 3.0, ((0, 16),), jnp.float32),
        "upstream": gaussian(key_of[9], (BR, FRAMES, FH, FW), 1.0, 6.0, ((0, 16), (1, 4))),
    }


void_class = 19

def column_band(offsets, widths, col_count):
    columns = jnp.arange(col_count, dtype=jnp.int32)
    return jnp.mod(columns[None, :] - offsets[:, None], col_count) < widths[:, None]

def swish_slope(value):
    sig = jax.nn.sigmoid(value)
    return sig * (1.0 + value * (1.0 - sig))

def reference(feats, offsets, widths, labels, dw_kernel, pw_weight, pw_bias, proj, proj_bias, upstream):
    frame_count, row_count, col_count, chan_count = feats.shape
    keep = column_band(offsets, widths, col_count).astype(jnp.bfloat16)
    masked = feats * keep[:, None, :, None]
    margin = RATE * (N_SECTION - 1)
    padded = jnp.pad(masked, ((0, 0), (margin, margin), (margin, margin), (0, 0)))
    pixel_count = frame_count * row_count * col_count
    labeled = (labels != void_class).reshape(pixel_count).astype(jnp.float32)
    scaling = 1.0 / math.sqrt(pixel_count)
    saved = []
    zsum = jnp.zeros((BR, pixel_count), jnp.float32)
    for segment_index in range(N_SECTION):
        dilation = RATE * segment_index
        kernel = dw_kernel[segment_index].astype(jnp.float32)
        accum = jnp.zeros((frame_count, row_count, col_count, chan_count), jnp.float32)
        for tap_index in range(9):
            row_step = tap_index // 3 - 1
            col_step = tap_index % 3 - 1
            top = margin + dilation * row_step
            left = margin + dilation * col_step
            accum = accum + padded[:, top:top + row_count, left:left + col_count, :].astype(jnp.float32) * kernel[tap_index]
        depth_out = accum.astype(jnp.bfloat16)
        depth_rows = depth_out.reshape(pixel_count, chan_count)
        preact = jnp.dot(pw_weight[segment_index].T, depth_rows.T, preferred_element_type=jnp.float32) + pw_bias[segment_index][:, None]
        branch_act = jax.nn.silu(preact).astype(jnp.bfloat16)
        zsum = zsum + jnp.dot(proj[segment_index].T, branch_act, preferred_element_type=jnp.float32)
        saved.append((depth_out, preact, branch_act))
    zvalue = zsum + proj_bias[:, None]
    aspp_out = jax.nn.silu(zvalue).astype(jnp.bfloat16).reshape(BR, frame_count, row_count, col_count)
    up_rows = upstream.reshape(BR, pixel_count).astype(jnp.float32)
    out_grad = (up_rows * swish_slope(zvalue) * labeled[None, :]).astype(jnp.bfloat16)
    grad_proj_bias = lax.optimization_barrier(jnp.sum(out_grad.astype(jnp.float32), axis=1)) * scaling
    input_sum = jnp.zeros((frame_count, row_count, col_count, chan_count), jnp.float32)
    grads_dw, grads_pw, grads_pwb, grads_proj = ([], [], [], [])
    for segment_index in range(N_SECTION):
        dilation = RATE * segment_index
        kernel = dw_kernel[segment_index].astype(jnp.float32)
        depth_out, preact, branch_act = saved[segment_index]
        depth_rows = depth_out.reshape(pixel_count, chan_count)
        act_grad = jnp.dot(proj[segment_index], out_grad, preferred_element_type=jnp.float32)
        grads_proj.append(jnp.dot(branch_act, out_grad.T, preferred_element_type=jnp.float32) * scaling)
        pre_grad = (act_grad * swish_slope(preact)).astype(jnp.bfloat16)
        grads_pwb.append(lax.optimization_barrier(jnp.sum(pre_grad.astype(jnp.float32), axis=1)) * scaling)
        grads_pw.append(jnp.dot(depth_rows.T, pre_grad.T, preferred_element_type=jnp.float32) * scaling)
        depth_grad = jnp.dot(pre_grad.T, pw_weight[segment_index].T, preferred_element_type=jnp.float32).astype(jnp.bfloat16)
        depth_grad = depth_grad.reshape(frame_count, row_count, col_count, chan_count)
        padded_grad = jnp.pad(depth_grad, ((0, 0), (margin, margin), (margin, margin), (0, 0)))
        depth_f = depth_grad.astype(jnp.float32)
        tap_grads = []
        for tap_index in range(9):
            row_step = tap_index // 3 - 1
            col_step = tap_index % 3 - 1
            top = margin + dilation * row_step
            left = margin + dilation * col_step
            source = padded[:, top:top + row_count, left:left + col_count, :].astype(jnp.float32)
            tap_grads.append(lax.optimization_barrier(jnp.sum(source * depth_f, axis=(0, 1, 2))) * scaling)
            top_back = margin - dilation * row_step
            left_back = margin - dilation * col_step
            shifted = padded_grad[:, top_back:top_back + row_count, left_back:left_back + col_count, :]
            input_sum = input_sum + shifted.astype(jnp.float32) * kernel[tap_index]
        grads_dw.append(jnp.stack(tap_grads))
    input_grad = (input_sum * keep[:, None, :, None].astype(jnp.float32)).astype(jnp.bfloat16)
    return (aspp_out, input_grad, jnp.stack(grads_dw), jnp.stack(grads_pw), jnp.stack(grads_pwb), jnp.stack(grads_proj), grad_proj_bias)
```

```python
import math

import jax
import jax.numpy as jnp
from jax import lax
from jax.experimental import pallas as pl
from jax.experimental.pallas import tpu as pltpu
from jax.sharding import Mesh, PartitionSpec as P

RATE = 6
VOID = 19
BF = jnp.bfloat16
F32 = jnp.float32

WIN = (32, 48, 48, 64)
BEG = (0, -8, -8, -16)
SOFF = (0, 32, 80, 128)
NCOL = 192
PADC = 32
PADR = 9
VM = 56 * 1024 * 1024


def shift(x, axis, k):
    n = lax.axis_size(axis)
    return lax.ppermute(x, axis, [(i, (i + k) % n) for i in range(n)])


def pick(x, i):
    return lax.dynamic_index_in_dim(x, i, 0, keepdims=False)


def exchange(x, axis):
    n = lax.axis_size(axis)
    me = lax.axis_index(axis)
    return [pick(x, me)] + [shift(pick(x, (me + k) % n), axis, k) for k in range(1, n)]


def gather_rel(x, axis):
    n = lax.axis_size(axis)
    return [x] + [shift(x, axis, k) for k in range(1, n)]


def in_order(parts, axis):
    n = lax.axis_size(axis)
    me = lax.axis_index(axis)
    return jnp.take(jnp.stack(parts), (me - jnp.arange(n)) % n, axis=0)


def dotf(a, b, dims=((1,), (0,))):
    return lax.dot_general(a, b, (dims, ((), ())), preferred_element_type=F32)


def select_kernel(sc, x, sel, *outs):
    for k in range(4):
        dest = lax.rem(sc[2] + k, 4)
        pick_mat = sel[dest]
        frame = dest // 2

        def body(t, _, k=k, pick_mat=pick_mat, frame=frame):
            outs[k][t] = dotf(pick_mat, x[frame, t, 0]).astype(BF)
            return 0

        lax.fori_loop(0, 16, body, 0, unroll=4)


def edge_masks(s, off, cp):
    n = WIN[s]
    u = lax.broadcasted_iota(jnp.int32, (n, 128), 0) + BEG[s]
    w = jnp.bitwise_and(off + 2 * u + cp, 127)
    return w >= RATE * s, w < 128 - RATE * s


def fill_x(xs, xscr):
    xscr[...] = jnp.zeros(xscr.shape, F32)
    for k in range(4):
        def body(t, _, k=k):
            xscr[k, PADR + t, PADC:PADC + 32, :] = xs[k][t].astype(F32)
            return 0
        lax.fori_loop(0, 16, body, 0, unroll=4)


def forward_kernel(sc, x0, x1, x2, x3, wb0, wb1, wb2, wb3, q0, q1, q2, q3,
                   depth, keep, send, wfull, dws, xscr, pscr):
    hf, off, cp, mc, mz, dp = sc[0], sc[3], sc[4], sc[5], sc[6], sc[7]
    fill_x((x0, x1, x2, x3), xscr)
    for k, wb in enumerate((wb0, wb1, wb2, wb3)):
        for s in range(4):
            dws[k, s] = wb[s, 32:48, 0:128].astype(F32)
    for r, qr in enumerate((q0, q1, q2, q3)):
        row = pl.multiple_of(32 * lax.rem(dp - r + 4, 4), 32)
        for k in range(4):
            for s in range(4):
                wfull[k, s, pl.ds(row, 32), :] = qr[k, s]

    def body(i, _):
        k = i // 8
        t = lax.rem(i, 8)
        base = 8 * hf + t + PADR
        total = jnp.sum(dws[k, 0, 0:9, :], axis=0, keepdims=True)
        depth[k, t, 0:32, :] = (xscr[k, base, PADC:PADC + 32, :] * total).astype(BF)
        for s in range(1, 4):
            n = WIN[s]
            parts = []
            for j in range(3):
                c0 = PADC + BEG[s] + 3 * s * (j - 1)
                acc = None
                for a in range(3):
                    v = xscr[k, base + 3 * s * (a - 1), c0:c0 + n, :] * dws[k, s, 3 * a + j:3 * a + j + 1, :]
                    acc = v if acc is None else acc + v
                parts.append(acc)
            left, right = edge_masks(s, off, cp)
            out = parts[1] + jnp.where(left, parts[0], 0.0) + jnp.where(right, parts[2], 0.0)
            depth[k, t, SOFF[s]:SOFF[s] + n, :] = out.astype(BF)
        return 0

    lax.fori_loop(0, 32, body, 0)
    for s in range(4):
        n = WIN[s]
        acc = None
        for k in range(0, 4, 2):
            lhs = jnp.concatenate(
                [depth[k + d, :, SOFF[s]:SOFF[s] + n, :].reshape(8 * n, 128) for d in range(2)], axis=1)
            rhs = jnp.concatenate([wfull[k, s], wfull[k + 1, s]], axis=0)
            v = dotf(lhs, rhs)
            acc = v if acc is None else acc + v
        pscr[:, SOFF[s]:SOFF[s] + n, :] = acc.reshape(8, n, 256)
    for zr in range(2):
        zz = 2 * jnp.bitwise_xor(mz, zr)
        for r in range(2):
            keep[zr, r] = pscr[4 * mc + zz + r]
            send[zr, r] = pscr[4 * (1 - mc) + zz + r].astype(BF)


def middle_kernel(sc, keep, rcore, rzl, pja, pjb, pjc, ups, lab,
                  res, pg, gp, pjs, upscr, gscr):
    mc, mz, zh = sc[5], sc[6], sc[2]
    for r in range(4):
        for cr in range(2):
            for zr in range(2):
                blk = 4 * lax.rem(zh - r + 4, 4) + 2 * jnp.bitwise_xor(mz, zr) + jnp.bitwise_xor(mc, cr)
                row = pl.multiple_of(16 * blk, 16)
                src = (pja if zr == 0 else pjb) if cr == 0 else pjc.at[zr]
                for s in range(4):
                    pjs[s, pl.ds(row, 16), :] = src[r, s]
                upscr[pl.ds(row, 16), :] = ups[cr, zr, r].astype(F32)
    lane = lax.broadcasted_iota(jnp.int32, (8, 128), 1)
    pre_now = keep[0] + rcore[0].astype(F32) + rzl[...].astype(F32)
    pres, acts = [], []
    z = dotf(jnp.where((lane >= 3) & (lane < 6), 1.0, 0.0).astype(BF), pjs[0, :, 256:384], ((1,), (1,)))[0:1, :]
    for s in range(4):
        n, v0 = WIN[s], BEG[s] + 16
        bias = dotf(jnp.where(lane < 3, 1.0, 0.0).astype(BF), pjs[s, :, 256:384], ((1,), (1,)))[0:1, :]
        body = pre_now[:, SOFF[s]:SOFF[s] + n, :]
        if n < 64:
            body = jnp.concatenate(
                [jnp.zeros((2, v0, 256), F32), body, jnp.zeros((2, 64 - n - v0, 256), F32)], axis=1)
        pre = body.reshape(128, 256) + bias
        act = (pre * jax.nn.sigmoid(pre)).astype(BF)
        z = z + dotf(act, pjs[s, :, 0:256])
        pres.append(pre)
        acts.append(act)
    sig = jax.nn.sigmoid(z)
    res_t = jnp.transpose(z * sig)
    up = jnp.transpose(upscr[...])
    og = (up * (sig * (1.0 + z * (1.0 - sig))) * lab[...]).astype(BF)
    ones = jnp.full((128, 128), 1.0, BF)
    half = lax.broadcasted_iota(jnp.int32, (256, 128), 1) < 64
    pbg = dotf(og, ones, ((0,), (0,)))
    for s in range(4):
        n, v0 = WIN[s], BEG[s] + 16
        pre = pres[s]
        sg = jax.nn.sigmoid(pre)
        ag = dotf(og, pjs[s, :, 0:256], ((1,), (1,)))
        pgs = (ag * (sg * (1.0 + pre * (1.0 - sg)))).astype(BF)
        pg[:, SOFF[s]:SOFF[s] + n, :] = pgs.reshape(2, 64, 256)[:, v0:v0 + n, :]
        gscr[s, :, 0:256] = dotf(acts[s], og, ((0,), (0,)))
        gscr[s, :, 256:384] = jnp.where(half, dotf(pgs, ones, ((0,), (0,))), pbg)
    upscr[...] = res_t
    for b in range(16):
        res[b] = upscr[16 * b:16 * b + 16, :].astype(BF)
    for r in range(4):
        for cr in range(2):
            for zr in range(2):
                blk = 4 * lax.rem(zh - r + 4, 4) + 2 * jnp.bitwise_xor(mz, zr) + jnp.bitwise_xor(mc, cr)
                row = pl.multiple_of(16 * blk, 16)
                for s in range(4):
                    gp[cr, zr, s, r] = gscr[s, pl.ds(row, 16), :]


def backward_kernel(sc, x0, x1, x2, x3, depth, wfull, dws, pga, pgb, pgc, gpr,
                    g0, g1, g2, g3, y0, y1, y2, y3, xscr, pgs, dgs, yscr, dwa, gbuf, ybuf):
    hf, q, off, cp, mc, mz = sc[0], sc[1], sc[3], sc[4], sc[5], sc[6]
    fill_x((x0, x1, x2, x3), xscr)
    for cr in range(2):
        for zr in range(2):
            t0 = 4 * jnp.bitwise_xor(mc, cr) + 2 * jnp.bitwise_xor(mz, zr)
            for r in range(2):
                if cr == 0:
                    pgs[t0 + r] = (pga if zr == 0 else pgb)[r]
                else:
                    pgs[t0 + r] = pgc[zr, r]
    for s in range(4):
        n = WIN[s]
        pg = pgs[:, SOFF[s]:SOFF[s] + n, :].reshape(8 * n, 256)
        for k in range(4):
            dep = depth[k, :, SOFF[s]:SOFF[s] + n, :].reshape(8 * n, 128)
            g = dotf(dep, pg, ((0,), (0,)))
            gbuf[s, k, 0:128, :] = g[:, 0:128].astype(BF)
            gbuf[s, k, 128:256, :] = g[:, 128:256].astype(BF)
            dgk = dotf(pg, wfull[k, s], ((1,), (1,))).astype(BF).astype(F32)
            dgs[k, :, SOFF[s]:SOFF[s] + n, :] = dgk.reshape(8, n, 128)
            for b in range(3):
                gbuf[s, k, 272 + 16 * b:288 + 16 * b, :] = gpr[s, k, :, 128 * b:128 * b + 128].astype(BF)
    yscr[...] = jnp.zeros(yscr.shape, F32)
    dwa[...] = jnp.zeros(dwa.shape, F32)

    def fold(v):
        n = v.shape[0]
        acc = v[0:8]
        for c in range(8, n, 8):
            acc = acc + v[c:c + 8]
        return acc

    def body(i, _):
        k = i // 8
        t = lax.rem(i, 8)
        base = 8 * hf + t + PADR
        d0 = dgs[k, t, 0:32, :]
        total = jnp.sum(dws[k, 0, 0:9, :], axis=0, keepdims=True)
        dwa[k, 0, 0:8, :] += fold(d0 * xscr[k, base, PADC:PADC + 32, :])
        yscr[k, t + PADR] += d0 * total
        for s in range(1, 4):
            n = WIN[s]
            left, right = edge_masks(s, off, cp)
            d = dgs[k, t, SOFF[s]:SOFF[s] + n, :]
            ds3 = (jnp.where(left, d, 0.0), d, jnp.where(right, d, 0.0))
            for a in range(3):
                for j in range(3):
                    c0 = PADC + BEG[s] + 3 * s * (j - 1)
                    v = fold(ds3[j] * xscr[k, base + 3 * s * (a - 1), c0:c0 + n, :])
                    tap = 9 * s + 3 * a + j - 8
                    dwa[k, tap, 0:8, :] += v
            acc = [None, None, None]
            for j in range(3):
                c1 = -BEG[s] - 3 * s * (j - 1)
                dv = ds3[j][c1:c1 + 32]
                for a in range(3):
                    v = dv * dws[k, s, 3 * a + j:3 * a + j + 1, :]
                    acc[a] = v if acc[a] is None else acc[a] + v
            for a in range(3):
                yscr[k, t + PADR + 3 * s * (a - 1)] += acc[a]
        return 0

    lax.fori_loop(0, 32, body, 0)
    for k in range(4):
        for s in range(4):
            rows = []
            for tap in range(9):
                src = 0 if s == 0 else 9 * s + tap - 8
                rows.append(jnp.sum(dwa[k, src], axis=0, keepdims=True))
            rows.append(jnp.zeros((7, 128), F32))
            gbuf[s, k, 256:272, :] = jnp.concatenate(rows, axis=0).astype(BF)
    outs = (g0, g1, g2, g3)
    youts = (y0, y1, y2, y3)
    for r in range(4):
        dest = lax.rem(q + r, 4)
        outs[r][...] = gbuf[dest]
        for k in range(4):
            for b in range(4):
                youts[r][k, b] = yscr[k, PADR - 8 * hf + 4 * dest + b].astype(BF)


def restore_kernel(sc, y0, y1, y2, y3, sel_t, out, yscr):
    zh, rp = sc[2], sc[8]
    for k, y in enumerate((y0, y1, y2, y3)):
        src = lax.rem(zh + k, 4)
        f, cp = src // 2, lax.rem(src, 2)
        for rho in range(2):
            for b in range(4):
                row = 2 * b + jnp.bitwise_xor(rp, rho)
                yscr[f, row, pl.ds(pl.multiple_of(32 * cp, 32), 32), :] = y[rho, b]
    for f in range(2):
        for h in range(8):
            out[f, h] = dotf(sel_t[f], yscr[f, h]).astype(BF)


def call(kernel, scalars, args, outs, scratch=(), in_specs=None, single=False):
    whole = pl.BlockSpec(memory_space=pltpu.VMEM)
    specs = in_specs if in_specs is not None else [whole] * len(args)
    return pl.pallas_call(
        kernel,
        grid_spec=pltpu.PrefetchScalarGridSpec(
            num_scalar_prefetch=1, grid=(1,), in_specs=specs,
            out_specs=[pl.BlockSpec(o[0], lambda i, sc, n=len(o[0]): (0,) * n) for o in outs],
            scratch_shapes=[pltpu.VMEM(s, d) for s, d in scratch]),
        out_shape=[jax.ShapeDtypeStruct(s, d) for s, d in outs],
        compiler_params=pltpu.CompilerParams(vmem_limit_bytes=VM),
    )(scalars, *args)


def split3(b):
    hi = b.astype(BF)
    rest = b - hi.astype(F32)
    mid = rest.astype(BF)
    low = (rest - mid.astype(F32)).astype(BF)
    return [hi, mid, low]


def local(feats, offsets, widths, labels, dw_kernel, pw_weight, pw_bias, proj, proj_bias, upstream):
    q = lax.axis_index("section")
    dp = lax.axis_index("dp")
    zh = lax.axis_index("zh")
    mz = lax.axis_index("zl")
    mc = lax.axis_index("core")
    hf, rp = q // 2, q % 2
    f, cp = zh // 2, zh % 2
    off = lax.dynamic_index_in_dim(offsets, f, 0, keepdims=False)
    scal = jnp.stack([hf, q, zh, off, cp, mc, mz, dp, rp]).astype(jnp.int32)
    scaling = 1.0 / math.sqrt(8192.0 * lax.axis_size("dp"))

    cols = jnp.arange(128, dtype=jnp.int32)
    rel = jnp.mod(cols[None, :] - offsets[:, None], 128)
    tgt = (2 * jnp.arange(32)[None, :] + jnp.arange(2)[:, None]).reshape(64)
    sel = ((rel[:, None, :] == tgt[None, :, None]) & (tgt[None, :] < widths[:, None])[:, :, None])
    ordv = jnp.mod(2 * (jnp.arange(64)[None, :] - 16) + jnp.arange(2)[:, None], 128).reshape(128)
    perm = (rel[:, :, None] == ordv[None, None, :])

    xs = call(
        select_kernel, scal, [feats.reshape(2, 16, 2, 128, 128), sel.astype(BF).reshape(4, 32, 128)],
        [((16, 32, 128), BF)] * 4,
        in_specs=[pl.BlockSpec((2, 16, 1, 128, 128), lambda i, sc: (0, 0, sc[8], 0, 0)),
                  pl.BlockSpec((4, 32, 128), lambda i, sc: (0, 0, 0))])
    xs = [xs[0]] + [shift(xs[k], "zh", k) for k in range(1, 4)]

    quarter = lax.dynamic_slice(pw_weight[0], (32 * dp, 0), (32, 256))
    taps = jnp.pad(dw_kernel[0], ((0, 7), (0, 128)))
    wblk = in_order(gather_rel(jnp.concatenate([quarter, taps], 0), "section"), "section")
    wbs = gather_rel(wblk, "zh")
    wq = jnp.stack([w[:, 0:32, :] for w in wbs])
    wqs = gather_rel(wq, "dp")

    extra = jnp.stack(split3(pw_bias[0]) + split3(proj_bias), axis=1)
    pblk = jnp.concatenate([proj[0], jnp.pad(extra, ((0, 0), (0, 122)))], axis=1)
    pblk = in_order(gather_rel(pblk, "section"), "section")
    pja = jnp.stack(gather_rel(pblk, "zh"))
    pjb = shift(pja, "zl", 1)
    pjc = shift(jnp.stack([pja, pjb]), "core", 1)

    upx = upstream.reshape(16, 2, 2, 8, 2, 128)
    upx = lax.dynamic_slice(upx, (0, 0, hf, 0, rp, 0), (16, 2, 1, 8, 1, 128)).reshape(16, 2, 8, 128)
    permb = perm.astype(BF)
    upr = jnp.einsum("cftw,fwx->fcxt", upx, permb, preferred_element_type=F32).astype(BF)
    upr = upr.reshape(2, 16, 2, 64, 2, 2, 2).transpose(0, 2, 4, 5, 1, 6, 3).reshape(4, 2, 2, 16, 128)
    ups = jnp.stack(exchange(upr, "zh"))
    ups = jnp.stack(exchange(jnp.moveaxis(ups, 2, 0), "zl"))
    ups = jnp.stack(exchange(jnp.moveaxis(ups, 2, 0), "core"))
    lab = lax.dynamic_slice(labels.reshape(2, 2, 2, 2, 2, 2, 128), (f, hf, mc, mz, 0, rp, 0),
                            (1, 1, 1, 1, 2, 1, 128)).reshape(2, 128)
    pm = lax.dynamic_slice(perm, (f, 0, 64 * cp), (1, 128, 64))[0].astype(F32)
    lab = jnp.dot((lab != VOID).astype(F32), pm).reshape(128, 1)

    depth, keep, send, wfull, dws = call(
        forward_kernel, scal, [*xs, *wbs, *wqs],
        [((4, 8, NCOL, 128), BF), ((2, 2, NCOL, 256), F32), ((2, 2, NCOL, 256), BF),
         ((4, 4, 128, 256), BF), ((4, 4, 16, 128), F32)],
        scratch=[((4, 34, 96, 128), F32), ((8, NCOL, 256), F32)])
    rcore = shift(send, "core", 1)
    rzl = shift((keep[1] + rcore[1].astype(F32)).astype(BF), "zl", 1)

    res, pga, gp = call(
        middle_kernel, scal, [keep, rcore, rzl, pja, pjb, pjc, ups, lab],
        [((16, 16, 128), BF), ((2, NCOL, 256), BF), ((2, 2, 4, 4, 16, 384), F32)],
        scratch=[((4, 256, 384), BF), ((256, 128), F32), ((4, 256, 384), F32)])

    pgb = shift(pga, "zl", 1)
    pgc = shift(jnp.stack([pga, pgb]), "core", 1)

    gz = gp[0] + shift(gp[1].astype(BF), "core", 1).astype(F32)
    gpr = gz[0] + shift(gz[1].astype(BF), "zl", 1).astype(F32)

    *gs, y0, y1, y2, y3 = call(
        backward_kernel, scal, [*xs, depth, wfull, dws, pga, pgb, pgc, gpr],
        [((4, 320, 128), BF)] * 4 + [((4, 4, 32, 128), BF)] * 4,
        scratch=[((4, 34, 96, 128), F32), ((8, NCOL, 256), BF), ((4, 8, NCOL, 128), F32),
                 ((4, 26, 32, 128), F32), ((4, 28, 8, 128), F32), ((4, 4, 320, 128), BF), ((8, 128), F32)])
    same = (y0.astype(F32) + shift(y2, "section", 2).astype(F32)).astype(BF)
    other = (shift(y1, "section", 1).astype(F32) + shift(y3, "section", 3).astype(F32)).astype(BF)
    yz = jnp.stack([same, other], axis=1)
    ys = [yz[0]] + [shift(yz[k], "zh", -k) for k in range(1, 4)]
    (input_grad,) = call(
        restore_kernel, scal, [*ys, jnp.swapaxes(sel, 1, 2).astype(BF)],
        [((2, 8, 128, 128), BF)], scratch=[((2, 8, 64, 128), BF)])

    gsum = gs[0].astype(F32)
    for k in range(1, 4):
        gsum = gsum + shift(gs[k], "section", k).astype(F32)
    gsb = gsum.astype(BF)
    gown = gsum[0]
    for k in range(1, 4):
        gown = gown + shift(gsb[k], "zh", -k).astype(F32)
    tot = gown
    for k in range(1, 4):
        tot = tot + shift(gown, "dp", k)
    tot = tot * scaling
    grad_pw = jnp.concatenate([tot[0:128], tot[128:256]], axis=1)
    grad_dw = tot[256:265]
    grad_proj = jnp.concatenate([tot[272:288], tot[288:304]], axis=1)
    grad_pwb = tot[304:320, 0]
    grad_pb = tot[304:320, 64]

    r6 = res.reshape(4, 2, 2, 16, 128)
    a = jnp.stack(exchange(jnp.moveaxis(r6, 2, 0), "core"))
    a = jnp.take(a, jnp.bitwise_xor(jnp.arange(2), mc), axis=0)
    a = jnp.stack(exchange(jnp.moveaxis(a, 2, 0), "zl"))
    a = jnp.take(a, jnp.bitwise_xor(jnp.arange(2), mz), axis=0)
    a = in_order(exchange(jnp.moveaxis(a, 2, 0), "zh"), "zh")
    a = a.reshape(2, 2, 2, 2, 16, 2, 64).transpose(0, 4, 3, 2, 5, 1, 6).reshape(2, 16, 8, 128)
    a = jnp.einsum("fctx,fwx->fctw", a, permb, preferred_element_type=F32).astype(BF)
    a = in_order(gather_rel(a, "section"), "section")
    aspp = a.reshape(2, 2, 2, 16, 8, 128).transpose(3, 2, 0, 4, 1, 5).reshape(16, 2, 32, 128)
    return (aspp, input_grad, grad_dw[None], grad_pw[None], grad_pwb[None], grad_proj[None], grad_pb)


def solution(mesh):
    fine = Mesh(mesh.devices.reshape(4, 4, 4, 2, 2), ("section", "dp", "zh", "zl", "core"))
    chan = ("zh", "zl", "core")
    in_specs = (
        P("dp", None, None, chan),
        P("dp"),
        P("dp"),
        P("dp", None, None),
        P("section", None, chan),
        P("section", chan, None),
        P("section", chan),
        P("section", chan, None),
        P(chan),
        P(chan, "dp", None, None),
    )
    out_specs = (
        P(chan, "dp", None, None),
        P("dp", "section", None, chan),
        P("section", None, chan),
        P("section", chan, None),
        P("section", chan),
        P("section", chan, None),
        P(chan),
    )
    return jax.shard_map(local, mesh=fine, in_specs=in_specs, out_specs=out_specs, check_vma=False)
```

```python
import math

import jax
import jax.numpy as jnp
from jax import lax
from jax.experimental import pallas as pl
from jax.experimental.pallas import tpu as pltpu
from jax.sharding import Mesh, PartitionSpec as P

RATE = 6
VOID = 19
BF = jnp.bfloat16
F32 = jnp.float32

WIN = (32, 48, 48, 64)
BEG = (0, -8, -8, -16)
SOFF = (0, 32, 80, 128)
NCOL = 192
PADC = 32
PADR = 9
VM = 56 * 1024 * 1024


def shift(x, axis, k):
    n = lax.axis_size(axis)
    return lax.ppermute(x, axis, [(i, (i + k) % n) for i in range(n)])


def gather_rel(x, axis):
    n = lax.axis_size(axis)
    return [x] + [shift(x, axis, k) for k in range(1, n)]


def dotf(a, b, dims=((1,), (0,))):
    return lax.dot_general(a, b, (dims, ((), ())), preferred_element_type=F32)


def back(a, k):
    return lax.rem(a - k + 4, 4)


def blocks(sc):
    for k in range(4):
        for zr in range(2):
            for cr in range(2):
                yield k, zr, cr, 4 * back(sc[2], k) + 2 * jnp.bitwise_xor(sc[3], zr) + jnp.bitwise_xor(sc[4], cr)


def perm_matrix(off, transpose=False):
    w = lax.broadcasted_iota(jnp.int32, (128, 128), 1 if transpose else 0)
    x = lax.broadcasted_iota(jnp.int32, (128, 128), 0 if transpose else 1)
    col = 2 * (jnp.bitwise_and(x, 63) - 16) + jnp.right_shift(x, 6)
    return jnp.where(jnp.bitwise_and(w - off, 127) == jnp.bitwise_and(col, 127), 1.0, 0.0).astype(BF)


def pack_kernel(sc, off, wid, pw, dw, proj, pwb, pb, out):
    rows = pl.ds(pl.multiple_of(32 * sc[5], 32), 32)
    out[0:32, :] = pw[0, rows, 0:128]
    out[32:64, :] = pw[0, rows, 128:256]
    out[64:80, :] = proj[0, :, 0:128]
    out[80:96, :] = proj[0, :, 128:256]
    i = lax.broadcasted_iota(jnp.int32, (16, 16), 0)
    j = lax.broadcasted_iota(jnp.int32, (16, 16), 1)
    lane = lax.broadcasted_iota(jnp.int32, (16, 128), 1)
    ext = jnp.zeros((16, 128), F32)
    for n, b in enumerate((pwb, pb)):
        rest = jnp.sum(jnp.where(i == j, b[...], 0.0), axis=1, keepdims=True)
        for piece in range(3):
            part = rest.astype(BF).astype(F32)
            ext = ext + jnp.where(lane == 3 * n + piece, part, 0.0)
            rest = rest - part
    out[96:112, :] = ext.astype(BF)
    taps = jnp.concatenate([dw[0].astype(F32), jnp.zeros((7, 128), F32)], axis=0)
    out[112:128, :] = taps.astype(BF)


def select_kernel(sc, off, wid, x, up, o0, o1, o2, o3, uscr):
    for f in range(2):
        res = dotf(up[f].reshape(128, 128), perm_matrix(off[f]))
        for p in range(2):
            uscr[2 * f + p] = res[:, 64 * p:64 * p + 64].reshape(8, 16, 64)
    for k, o in enumerate((o0, o1, o2, o3)):
        dest = lax.rem(sc[2] + k, 4)
        f, p = dest // 2, lax.rem(dest, 2)
        w = lax.broadcasted_iota(jnp.int32, (32, 128), 1)
        tgt = 2 * lax.broadcasted_iota(jnp.int32, (32, 128), 0) + p
        hot = jnp.where((jnp.bitwise_and(w - off[f], 127) == tgt) & (tgt < wid[f]), 1.0, 0.0).astype(BF)

        def body(t, _, o=o, hot=hot, f=f):
            o[pl.ds(pl.multiple_of(32 * t, 32), 32), :] = dotf(hot, x[f, t, 0]).astype(BF)
            return 0

        lax.fori_loop(0, 16, body, 0, unroll=8)
        for zr in range(2):
            for cr in range(2):
                t0 = 4 * jnp.bitwise_xor(sc[4], cr) + 2 * jnp.bitwise_xor(sc[3], zr)
                row = 512 + 32 * zr + 16 * cr
                o[row:row + 16, :] = jnp.concatenate([uscr[dest, t0], uscr[dest, t0 + 1]], axis=1).astype(BF)


def edge_masks(s, off, cp):
    n = WIN[s]
    u = lax.broadcasted_iota(jnp.int32, (n, 128), 0) + BEG[s]
    w = jnp.bitwise_and(off + 2 * u + cp, 127)
    return w >= RATE * s, w < 128 - RATE * s


def fill_x(xs, xscr):
    xscr[...] = jnp.zeros(xscr.shape, F32)
    for k in range(4):
        def body(t, _, k=k):
            xscr[k, PADR + t, PADC:PADC + 32, :] = xs[k][pl.ds(pl.multiple_of(32 * t, 32), 32), :].astype(F32)
            return 0
        lax.fori_loop(0, 16, body, 0, unroll=4)


def depth_kernel(sc, off, wid, x0, x1, x2, x3, a0, a1, a2, a3, depth, dws, xscr):
    hf, f, cp = sc[0], sc[2] // 2, lax.rem(sc[2], 2)
    col = off[f]
    fill_x((x0, x1, x2, x3), xscr)
    for k, a in enumerate((a0, a1, a2, a3)):
        for r in range(4):
            dws[k, back(sc[1], r)] = a[r, 112:128, :].astype(F32)

    def body(i, _):
        k = i // 8
        t = lax.rem(i, 8)
        base = 8 * hf + t + PADR
        total = jnp.sum(dws[k, 0, 0:9, :], axis=0, keepdims=True)
        depth[k, t, 0:32, :] = (xscr[k, base, PADC:PADC + 32, :] * total).astype(BF)
        for s in range(1, 4):
            n = WIN[s]
            parts = []
            for j in range(3):
                c0 = PADC + BEG[s] + 3 * s * (j - 1)
                acc = None
                for a in range(3):
                    v = xscr[k, base + 3 * s * (a - 1), c0:c0 + n, :] * dws[k, s, 3 * a + j:3 * a + j + 1, :]
                    acc = v if acc is None else acc + v
                parts.append(acc)
            left, right = edge_masks(s, col, cp)
            out = parts[1] + jnp.where(left, parts[0], 0.0) + jnp.where(right, parts[2], 0.0)
            depth[k, t, SOFF[s]:SOFF[s] + n, :] = out.astype(BF)
        return 0

    lax.fori_loop(0, 32, body, 0)


def product_kernel(sc, off, wid, depth, q0, q1, q2, q3, keep, send, wfull, pscr):
    mz, mc = sc[3], sc[4]
    for j, qj in enumerate((q0, q1, q2, q3)):
        rows = pl.ds(pl.multiple_of(32 * back(sc[5], j), 32), 32)
        for k in range(4):
            for r in range(4):
                s = back(sc[1], r)
                wfull[k, s, rows, 0:128] = qj[k, r, 0:32, :]
                wfull[k, s, rows, 128:256] = qj[k, r, 32:64, :]
    for s in range(4):
        n = WIN[s]
        acc = None
        for k in range(0, 4, 2):
            lhs = jnp.concatenate(
                [depth[k + d, :, SOFF[s]:SOFF[s] + n, :].reshape(8 * n, 128) for d in range(2)], axis=1)
            rhs = jnp.concatenate([wfull[k, s], wfull[k + 1, s]], axis=0)
            v = dotf(lhs, rhs)
            acc = v if acc is None else acc + v
        pscr[:, SOFF[s]:SOFF[s] + n, :] = acc.reshape(8, n, 256)
    for zr in range(2):
        zz = 2 * jnp.bitwise_xor(mz, zr)
        for r in range(2):
            keep[zr, r] = pscr[4 * mc + zz + r]
            send[zr, r] = pscr[4 * (1 - mc) + zz + r].astype(BF)


def middle_kernel(sc, off, wid, keep, rcore, rzl, pj, zin, cin, f0, f1, f2, f3, labels,
                  zout, res0, gkeep, gsend, pjs, upscr, gscr):
    q, zh, mz, mc = sc[1], sc[2], sc[3], sc[4]
    fs = (f0, f1, f2, f3)
    for k, zr, cr, blk in blocks(sc):
        rows = pl.ds(pl.multiple_of(16 * blk, 16), 16)
        for r in range(4):
            s = back(q, r)
            base = 48 * (4 * k + r)
            for b in range(3):
                at = base + 16 * b
                if zr == 0 and cr == 0:
                    v = pj[k, r, 16 * b:16 * b + 16, :]
                elif cr == 0:
                    v = zin[at:at + 16, :]
                else:
                    v = cin[768 * zr + at:768 * zr + at + 16, :]
                pjs[s, rows, 128 * b:128 * b + 128] = v
        if zr == 0 and cr == 0:
            u = fs[k][512:528, :]
        elif cr == 0:
            u = zin[768 + 32 * k:784 + 32 * k, :]
        else:
            u = cin[1536 + 64 * zr + 16 * k:1552 + 64 * zr + 16 * k, :]
        upscr[rows, :] = u.astype(F32)
    frame, cp = zh // 2, lax.rem(zh, 2)
    w = lax.broadcasted_iota(jnp.int32, (64, 128), 1)
    v = lax.broadcasted_iota(jnp.int32, (64, 128), 0)
    hot = jnp.bitwise_and(w - off[frame], 127) == jnp.bitwise_and(2 * (v - 16) + cp, 127)
    cols = []
    for r in range(2):
        row = 2 * (8 * sc[0] + 4 * mc + 2 * mz + r) + sc[6]
        lrow = labels[frame, pl.ds(row, 1), :]
        cols.append(jnp.sum(jnp.where(hot & (lrow != VOID), 1.0, 0.0), axis=1, keepdims=True))
    lab = jnp.concatenate(cols, axis=0)

    lane = lax.broadcasted_iota(jnp.int32, (8, 128), 1)
    pre_now = keep[0] + rcore[0].astype(F32) + rzl[...].astype(F32)
    pres, acts = [], []
    z = dotf(jnp.where((lane >= 3) & (lane < 6), 1.0, 0.0).astype(BF), pjs[0, :, 256:384], ((1,), (1,)))[0:1, :]
    for s in range(4):
        n, v0 = WIN[s], BEG[s] + 16
        bias = dotf(jnp.where(lane < 3, 1.0, 0.0).astype(BF), pjs[s, :, 256:384], ((1,), (1,)))[0:1, :]
        body = pre_now[:, SOFF[s]:SOFF[s] + n, :]
        if n < 64:
            body = jnp.concatenate(
                [jnp.zeros((2, v0, 256), F32), body, jnp.zeros((2, 64 - n - v0, 256), F32)], axis=1)
        pre = body.reshape(128, 256) + bias
        act = (pre * jax.nn.sigmoid(pre)).astype(BF)
        z = z + dotf(act, pjs[s, :, 0:256])
        pres.append(pre)
        acts.append(act)
    sig = jax.nn.sigmoid(z)
    res_t = jnp.transpose(z * sig)
    up = jnp.transpose(upscr[...])
    og = (up * (sig * (1.0 + z * (1.0 - sig))) * lab).astype(BF)
    ones = jnp.full((128, 128), 1.0, BF)
    half = lax.broadcasted_iota(jnp.int32, (256, 128), 1) < 64
    pbg = dotf(og, ones, ((0,), (0,)))
    for s in range(4):
        n, v0 = WIN[s], BEG[s] + 16
        pre = pres[s]
        sg = jax.nn.sigmoid(pre)
        ag = dotf(og, pjs[s, :, 0:256], ((1,), (1,)))
        pgs = (ag * (sg * (1.0 + pre * (1.0 - sg)))).astype(BF)
        for b in range(2):
            for r in range(2):
                at = 384 * b + 192 * r + SOFF[s]
                zout[at:at + n, :] = pgs[64 * r + v0:64 * r + v0 + n, 128 * b:128 * b + 128]
        gscr[s, :, 0:256] = dotf(acts[s], og, ((0,), (0,)))
        gscr[s, :, 256:384] = jnp.where(half, dotf(pgs, ones, ((0,), (0,))), pbg)
    upscr[...] = res_t
    for k, zr, cr, blk in blocks(sc):
        rows = pl.ds(pl.multiple_of(16 * blk, 16), 16)
        at = 64 * cr + 16 * k
        if zr == 0:
            res0[at:at + 16, :] = upscr[rows, :].astype(BF)
        else:
            zout[768 + at:784 + at, :] = upscr[rows, :].astype(BF)
        for r in range(4):
            g = gscr[lax.rem(q + r, 4), rows, :]
            if cr == 0:
                gkeep[zr, r, k] = g
            else:
                gsend[zr, r, k] = g.astype(BF)


def weight_kernel(sc, off, wid, depth, zout, zin, cin, g0, g1, g2, g3, pgs, gbuf):
    mz, mc = sc[3], sc[4]
    for zr in range(2):
        for cr in range(2):
            t0 = 4 * jnp.bitwise_xor(mc, cr) + 2 * jnp.bitwise_xor(mz, zr)
            src, at0 = (cin, 768 * zr) if cr == 1 else ((zout, 0) if zr == 0 else (zin, 0))
            for r in range(2):
                for b in range(2):
                    at = at0 + 384 * b + 192 * r
                    pgs[t0 + r, :, 128 * b:128 * b + 128] = src[at:at + 192, :]
    for s in range(4):
        n = WIN[s]
        pg = pgs[:, SOFF[s]:SOFF[s] + n, :].reshape(8 * n, 256)
        for k in range(4):
            dep = depth[k, :, SOFF[s]:SOFF[s] + n, :].reshape(8 * n, 128)
            g = dotf(dep, pg, ((0,), (0,)))
            gbuf[s, k, 0:128, :] = g[:, 0:128].astype(BF)
            gbuf[s, k, 128:256, :] = g[:, 128:256].astype(BF)
    for r, g in enumerate((g0, g1, g2, g3)):
        g[...] = gbuf[lax.rem(sc[1] + r, 4)]


def backward_kernel(sc, off, wid, x0, x1, x2, x3, wfull, dws, pgs, gpr, res0, zin, cin,
                    o0, o1, o2, o3, xscr, dgs, yscr, dwa):
    hf, q, f, cp = sc[0], sc[1], sc[2] // 2, lax.rem(sc[2], 2)
    col = off[f]
    fill_x((x0, x1, x2, x3), xscr)
    for s in range(4):
        n = WIN[s]
        pg = pgs[:, SOFF[s]:SOFF[s] + n, :].reshape(8 * n, 256)
        for k in range(4):
            dgk = dotf(pg, wfull[k, s], ((1,), (1,))).astype(BF).astype(F32)
            dgs[k, :, SOFF[s]:SOFF[s] + n, :] = dgk.reshape(8, n, 128)
    yscr[...] = jnp.zeros(yscr.shape, F32)
    dwa[...] = jnp.zeros(dwa.shape, F32)

    def fold(v):
        n = v.shape[0]
        acc = v[0:8]
        for c in range(8, n, 8):
            acc = acc + v[c:c + 8]
        return acc

    def body(i, _):
        k = i // 8
        t = lax.rem(i, 8)
        base = 8 * hf + t + PADR
        d0 = dgs[k, t, 0:32, :]
        total = jnp.sum(dws[k, 0, 0:9, :], axis=0, keepdims=True)
        dwa[k, 0, 0:8, :] += fold(d0 * xscr[k, base, PADC:PADC + 32, :])
        yscr[k, t + PADR] += d0 * total
        for s in range(1, 4):
            n = WIN[s]
            left, right = edge_masks(s, col, cp)
            d = dgs[k, t, SOFF[s]:SOFF[s] + n, :]
            ds3 = (jnp.where(left, d, 0.0), d, jnp.where(right, d, 0.0))
            for a in range(3):
                for j in range(3):
                    c0 = PADC + BEG[s] + 3 * s * (j - 1)
                    v = fold(ds3[j] * xscr[k, base + 3 * s * (a - 1), c0:c0 + n, :])
                    tap = 9 * s + 3 * a + j - 8
                    dwa[k, tap, 0:8, :] += v
            acc = [None, None, None]
            for j in range(3):
                c1 = -BEG[s] - 3 * s * (j - 1)
                dv = ds3[j][c1:c1 + 32]
                for a in range(3):
                    v = dv * dws[k, s, 3 * a + j:3 * a + j + 1, :]
                    acc[a] = v if acc[a] is None else acc[a] + v
            for a in range(3):
                yscr[k, t + PADR + 3 * s * (a - 1)] += acc[a]
        return 0

    lax.fori_loop(0, 32, body, 0)
    for k in range(4):
        for s in range(4):
            rows = []
            for tap in range(9):
                src = 0 if s == 0 else 9 * s + tap - 8
                rows.append(jnp.sum(dwa[k, src], axis=0, keepdims=True))
            rows.append(jnp.zeros((7, 128), F32))
            dws_sum = jnp.concatenate(rows, axis=0)
            dwa[k, 28 + 2 * s] = dws_sum[0:8]
            dwa[k, 29 + 2 * s] = dws_sum[8:16]
    for r, o in enumerate((o0, o1, o2, o3)):
        dest = lax.rem(q + r, 4)
        for k in range(4):
            for b in range(4):
                at = 128 * k + 32 * b
                o[at:at + 32, :] = yscr[k, PADR - 8 * hf + 4 * dest + b].astype(BF)
            o[512 + 16 * k:528 + 16 * k, :] = jnp.concatenate(
                [dwa[k, 28 + 2 * dest], dwa[k, 29 + 2 * dest]], axis=0).astype(BF)
            for b in range(3):
                at = 576 + 48 * k + 16 * b
                o[at:at + 16, :] = gpr[r, k, :, 128 * b:128 * b + 128].astype(BF)
        o[768:832, :] = res0[0:64, :]
        o[832:896, :] = cin[1536:1600, :]
        o[896:960, :] = zin[768:832, :]
        o[960:1024, :] = cin[1600:1664, :]


def combine_kernel(v0, v1, v2, v3, o0, o1, o2, o3):
    vs = (v0, v1, v2, v3)
    for k, o in enumerate((o0, o1, o2, o3)):
        ys = slice(128 * k, 128 * k + 128)
        o[0:128, :] = (v0[ys, :].astype(F32) + v2[ys, :].astype(F32)).astype(BF)
        o[128:256, :] = (v1[ys, :].astype(F32) + v3[ys, :].astype(F32)).astype(BF)
        for at, src, n in ((256, 512 + 16 * k, 16), (272, 576 + 48 * k, 48)):
            tot = v0[src:src + n, :].astype(F32)
            for v in vs[1:]:
                tot = tot + v[src:src + n, :].astype(F32)
            o[at:at + n, :] = tot.astype(BF)
        for r, v in enumerate(vs):
            for b in range(4):
                at = 320 + 64 * r + 16 * b
                o[at:at + 16, :] = v[768 + 64 * b + 16 * k:784 + 64 * b + 16 * k, :]


def restore_kernel(sc, off, wid, z0, z1, z2, z3, out, asp, small, zs, yscr, ascr):
    q, zh, mz, mc, rp = sc[1], sc[2], sc[3], sc[4], sc[6]
    tot = None
    for k, z in enumerate((z0, z1, z2, z3)):
        src = lax.rem(zh + k, 4)
        zs[src] = z[...]
        v = z[256:320, :].astype(F32)
        tot = v if tot is None else tot + v
    small[...] = tot
    for f in range(2):
        w = lax.broadcasted_iota(jnp.int32, (128, 64), 0)
        x = lax.broadcasted_iota(jnp.int32, (128, 64), 1)
        tgt = 2 * jnp.bitwise_and(x, 31) + jnp.right_shift(x, 5)
        hot = jnp.where((jnp.bitwise_and(w - off[f], 127) == tgt) & (tgt < wid[f]), 1.0, 0.0).astype(BF)
        for rho in range(2):
            par = jnp.bitwise_xor(rp, rho)
            for b in range(4):
                at = 128 * rho + 32 * b
                both = jnp.concatenate([zs[2 * f, at:at + 32, :], zs[2 * f + 1, at:at + 32, :]], axis=0)
                out[f, 2 * b + par] = dotf(hot, both).astype(BF)
        for r in range(4):
            qs = back(q, r)
            for zr in range(2):
                for cr in range(2):
                    t0 = 8 * (qs // 2) + 4 * jnp.bitwise_xor(mc, cr) + 2 * jnp.bitwise_xor(mz, zr)
                    at = 320 + 64 * r + 32 * zr + 16 * cr
                    for e in range(2):
                        h = 2 * (t0 + e) + lax.rem(qs, 2)
                        ascr[h] = jnp.concatenate(
                            [zs[2 * f, at:at + 16, 64 * e:64 * e + 64],
                             zs[2 * f + 1, at:at + 16, 64 * e:64 * e + 64]], axis=1)
        asp[f] = dotf(ascr[...].reshape(512, 128), perm_matrix(off[f], True)).astype(BF).reshape(32, 16, 128)


def call(kernel, scalars, args, outs, scratch=(), in_specs=None):
    whole = pl.BlockSpec(memory_space=pltpu.VMEM)
    specs = in_specs if in_specs is not None else [whole] * len(args)
    return pl.pallas_call(
        kernel,
        grid_spec=pltpu.PrefetchScalarGridSpec(
            num_scalar_prefetch=len(scalars), grid=(1,), in_specs=specs,
            out_specs=[pl.BlockSpec(o[0], lambda *a, n=len(o[0]): (0,) * n) for o in outs],
            scratch_shapes=[pltpu.VMEM(s, d) for s, d in scratch]),
        out_shape=[jax.ShapeDtypeStruct(s, d) for s, d in outs],
        compiler_params=pltpu.CompilerParams(vmem_limit_bytes=VM),
    )(*scalars, *args)


def local(feats, offsets, widths, labels, dw_kernel, pw_weight, pw_bias, proj, proj_bias, upstream):
    q = lax.axis_index("section")
    hf, rp = q // 2, q % 2
    scal = jnp.stack([hf, q, lax.axis_index("zh"), lax.axis_index("zl"), lax.axis_index("core"),
                      lax.axis_index("dp"), rp]).astype(jnp.int32)
    sc = (scal, offsets, widths)
    scaling = 1.0 / math.sqrt(8192.0 * lax.axis_size("dp"))

    (blk,) = call(pack_kernel, sc, [pw_weight, dw_kernel, proj, pw_bias, proj_bias[None]], [((128, 128), BF)])
    wz = gather_rel(jnp.stack(gather_rel(blk, "section")), "zh")
    quarters = gather_rel(jnp.stack([a[:, 0:64] for a in wz]), "dp")

    upx = upstream.reshape(16, 2, 2, 8, 2, 128)
    upx = lax.dynamic_slice(upx, (0, 0, hf, 0, rp, 0), (16, 2, 1, 8, 1, 128)).reshape(16, 2, 8, 128)
    upx = upx.transpose(1, 2, 0, 3)
    xs = call(
        select_kernel, sc, [feats.reshape(2, 16, 2, 128, 128), upx], [((576, 128), BF)] * 4,
        scratch=[((4, 8, 16, 64), F32)],
        in_specs=[pl.BlockSpec((2, 16, 1, 128, 128), lambda i, sc, off, wid: (0, 0, sc[6], 0, 0)),
                  pl.BlockSpec((2, 8, 16, 128), lambda i, *a: (0, 0, 0, 0))])
    xs = [xs[0]] + [shift(xs[k], "zh", k) for k in range(1, 4)]

    depth, dws = call(
        depth_kernel, sc, [*xs, *wz], [((4, 8, NCOL, 128), BF), ((4, 4, 16, 128), F32)],
        scratch=[((4, 34, 96, 128), F32)])
    keep, send, wfull = call(
        product_kernel, sc, [depth, *quarters],
        [((2, 2, NCOL, 256), F32), ((2, 2, NCOL, 256), BF), ((4, 4, 128, 256), BF)],
        scratch=[((8, NCOL, 256), F32)])

    pj = jnp.stack([a[:, 64:112] for a in wz])
    pjflat = pj.reshape(768, 128)
    uz = shift(jnp.concatenate([pjflat] + [x[544:576] for x in xs], axis=0), "zl", 1)
    uc = shift(jnp.concatenate(
        [pjflat, uz[0:768]] + [x[528:544] for x in xs] + [uz[784 + 32 * k:800 + 32 * k] for k in range(4)],
        axis=0), "core", 1)

    rcore = shift(send, "core", 1)
    rzl = shift((keep[1] + rcore[1].astype(F32)).astype(BF), "zl", 1)
    zout, res0, gkeep, gsend = call(
        middle_kernel, sc, [keep, rcore, rzl, pj, uz, uc, *xs, labels],
        [((896, 128), BF), ((128, 128), BF), ((2, 4, 4, 16, 384), F32), ((2, 4, 4, 16, 384), BF)],
        scratch=[((4, 256, 384), BF), ((256, 128), F32), ((4, 256, 384), F32)])

    zin = shift(zout, "zl", 1)
    cin = shift(jnp.concatenate([zout[0:768], zin[0:768], res0[64:128], zin[832:896]], axis=0), "core", 1)
    gz = gkeep + shift(gsend, "core", 1).astype(F32)
    gpr = gz[0] + shift(gz[1].astype(BF), "zl", 1).astype(F32)

    *gs, pgs = call(
        weight_kernel, sc, [depth, zout, zin, cin], [((4, 256, 128), BF)] * 4 + [((8, NCOL, 256), BF)],
        scratch=[((4, 4, 256, 128), BF)])
    vs = call(
        backward_kernel, sc, [*xs, wfull, dws, pgs, gpr, res0, zin, cin], [((1024, 128), BF)] * 4,
        scratch=[((4, 34, 96, 128), F32), ((4, 8, NCOL, 128), F32), ((4, 26, 32, 128), F32), ((4, 36, 8, 128), F32)])

    gsum = gs[0].astype(F32)
    for k in range(1, 4):
        gsum = gsum + shift(gs[k], "section", k).astype(F32)
    gsb = gsum.astype(BF)
    gown = gsum[0]
    for k in range(1, 4):
        gown = gown + shift(gsb[k], "zh", -k).astype(F32)

    zs = call(combine_kernel, (), [vs[0]] + [shift(vs[k], "section", k) for k in range(1, 4)],
              [((576, 128), BF)] * 4)
    input_grad, asp, small = call(
        restore_kernel, sc, [zs[0]] + [shift(zs[k], "zh", -k) for k in range(1, 4)],
        [((2, 8, 128, 128), BF), ((2, 32, 16, 128), BF), ((64, 128), F32)],
        scratch=[((4, 576, 128), BF), ((8, 128), F32), ((32, 16, 128), BF)])

    own = jnp.concatenate([gown, small], axis=0)
    ownb = own.astype(BF)
    tot = own
    for k in range(1, 4):
        tot = tot + shift(ownb, "dp", k).astype(F32)
    tot = tot * scaling
    grad_pw = jnp.concatenate([tot[0:128], tot[128:256]], axis=1)
    grad_dw = tot[256:265]
    grad_proj = jnp.concatenate([tot[272:288], tot[288:304]], axis=1)
    grad_pwb = tot[304:320, 0]
    grad_pb = tot[304:320, 64]
    aspp = asp.transpose(2, 0, 1, 3)
    return (aspp, input_grad, grad_dw[None], grad_pw[None], grad_pwb[None], grad_proj[None], grad_pb)


def solution(mesh):
    fine = Mesh(mesh.devices.reshape(4, 4, 4, 2, 2), ("section", "dp", "zh", "zl", "core"))
    chan = ("zh", "zl", "core")
    in_specs = (
        P("dp", None, None, chan),
        P("dp"),
        P("dp"),
        P("dp", None, None),
        P("section", None, chan),
        P("section", chan, None),
        P("section", chan),
        P("section", chan, None),
        P(chan),
        P(chan, "dp", None, None),
    )
    out_specs = (
        P(chan, "dp", None, None),
        P("dp", "section", None, chan),
        P("section", None, chan),
        P("section", chan, None),
        P("section", chan),
        P("section", chan, None),
        P(chan),
    )
    return jax.shard_map(local, mesh=fine, in_specs=in_specs, out_specs=out_specs, check_vma=False)
```

```python
import functools
import math

import jax
import jax.numpy as jnp
from jax import lax
from jax.experimental import pallas as pl
from jax.experimental.pallas import tpu as pltpu
from jax.sharding import Mesh, PartitionSpec as P

RATE = 6
VOID = 19
BF = jnp.bfloat16
F32 = jnp.float32

WIN = (32, 48, 48, 64)
BEG = (0, -8, -8, -16)
SOFF = (0, 32, 80, 128)
NCOL = 192
PADC = 32
PADR = 9
VM = 56 * 1024 * 1024


def shift(x, axis, k):
    n = lax.axis_size(axis)
    return lax.ppermute(x, axis, [(i, (i + k) % n) for i in range(n)])


def gather_rel(x, axis):
    n = lax.axis_size(axis)
    return [x] + [shift(x, axis, k) for k in range(1, n)]


def dotf(a, b, dims=((1,), (0,))):
    return lax.dot_general(a, b, (dims, ((), ())), preferred_element_type=F32)


def back(a, k):
    return lax.rem(a - k + 4, 4)


def blocks(sc):
    for k in range(4):
        for zr in range(2):
            for cr in range(2):
                yield k, zr, cr, 4 * back(sc[2], k) + 2 * jnp.bitwise_xor(sc[3], zr) + jnp.bitwise_xor(sc[4], cr)


def perm_matrix(off, transpose=False):
    w = lax.broadcasted_iota(jnp.int32, (128, 128), 1 if transpose else 0)
    x = lax.broadcasted_iota(jnp.int32, (128, 128), 0 if transpose else 1)
    col = 2 * (jnp.bitwise_and(x, 63) - 16) + jnp.right_shift(x, 6)
    return jnp.where(jnp.bitwise_and(w - off, 127) == jnp.bitwise_and(col, 127), 1.0, 0.0).astype(BF)


def pack_kernel(sc, off, wid, pw, dw, proj, pwb, pb, out):
    rows = pl.ds(pl.multiple_of(32 * sc[5], 32), 32)
    out[0:32, :] = pw[0, rows, 0:128]
    out[32:64, :] = pw[0, rows, 128:256]
    out[80:96, :] = proj[0, :, 0:128]
    out[96:112, :] = proj[0, :, 128:256]
    i = lax.broadcasted_iota(jnp.int32, (16, 16), 0)
    j = lax.broadcasted_iota(jnp.int32, (16, 16), 1)
    lane = lax.broadcasted_iota(jnp.int32, (16, 128), 1)
    ext = jnp.zeros((16, 128), F32)
    for n, b in enumerate((pwb, pb)):
        rest = jnp.sum(jnp.where(i == j, b[...], 0.0), axis=1, keepdims=True)
        for piece in range(3):
            part = rest.astype(BF).astype(F32)
            ext = ext + jnp.where(lane == 3 * n + piece, part, 0.0)
            rest = rest - part
    out[112:128, :] = ext.astype(BF)
    taps = jnp.concatenate([dw[0].astype(F32), jnp.zeros((7, 128), F32)], axis=0)
    out[64:80, :] = taps.astype(BF)


def branch_kernel(sc, off, wid, b0, b1, b2, b3, out):
    for r, b in enumerate((b0, b1, b2, b3)):
        out[64 * r:64 * r + 64, :] = b[0:64, :]
        out[304 + 16 * r:320 + 16 * r, :] = b[64:80, :]

        @pl.when(sc[5] == r)
        def _(b=b):
            out[256:304, :] = b[80:128, :]


def proj_kernel(sc, off, wid, q0, q1, q2, q3, own, wfull):
    for j, qj in enumerate((q0, q1, q2, q3)):
        d = back(sc[5], j)
        lanes = pl.ds(pl.multiple_of(32 * d, 32), 32)
        for k in range(4):
            for r in range(4):
                s = back(sc[1], r)
                for b in range(2):
                    at = 304 * k + 64 * r + 32 * b
                    wfull[k, s, lanes, 128 * b:128 * b + 128] = qj[at:at + 32, :]
            at = 304 * k + 256
            own[pl.ds(pl.multiple_of(192 * k + 48 * d, 16), 48), :] = qj[at:at + 48, :]


def select_kernel(sc, off, wid, x, up, o0, o1, o2, o3, uscr):
    for f in range(2):
        res = dotf(up[f].reshape(128, 128), perm_matrix(off[f]))
        for p in range(2):
            uscr[2 * f + p] = res[:, 64 * p:64 * p + 64].reshape(8, 16, 64)
    for k, o in enumerate((o0, o1, o2, o3)):
        dest = lax.rem(sc[2] + k, 4)
        f, p = dest // 2, lax.rem(dest, 2)
        w = lax.broadcasted_iota(jnp.int32, (32, 128), 1)
        tgt = 2 * lax.broadcasted_iota(jnp.int32, (32, 128), 0) + p
        hot = jnp.where((jnp.bitwise_and(w - off[f], 127) == tgt) & (tgt < wid[f]), 1.0, 0.0).astype(BF)

        def body(t, _, o=o, hot=hot, f=f):
            o[pl.ds(pl.multiple_of(32 * t, 32), 32), :] = dotf(hot, x[f, t, 0]).astype(BF)
            return 0

        lax.fori_loop(0, 16, body, 0, unroll=8)
        for zr in range(2):
            for cr in range(2):
                t0 = 4 * jnp.bitwise_xor(sc[4], cr) + 2 * jnp.bitwise_xor(sc[3], zr)
                row = 512 + 32 * zr + 16 * cr
                o[row:row + 16, :] = jnp.concatenate([uscr[dest, t0], uscr[dest, t0 + 1]], axis=1).astype(BF)


def edge_masks(s, off, cp):
    n = WIN[s]
    u = lax.broadcasted_iota(jnp.int32, (n, 128), 0) + BEG[s]
    w = jnp.bitwise_and(off + 2 * u + cp, 127)
    return w >= RATE * s, w < 128 - RATE * s


def fill_x(xs, xscr):
    xscr[...] = jnp.zeros(xscr.shape, F32)
    for k in range(4):
        def body(t, _, k=k):
            xscr[k, PADR + t, PADC:PADC + 32, :] = xs[k][pl.ds(pl.multiple_of(32 * t, 32), 32), :].astype(F32)
            return 0
        lax.fori_loop(0, 16, body, 0, unroll=4)


def depth_kernel(sc, off, wid, x0, x1, x2, x3, a0, a1, a2, a3, depth, dws, xscr):
    hf, f, cp = sc[0], sc[2] // 2, lax.rem(sc[2], 2)
    col = off[f]
    fill_x((x0, x1, x2, x3), xscr)
    for k, a in enumerate((a0, a1, a2, a3)):
        for r in range(4):
            dws[k, back(sc[1], r)] = a[304 + 16 * r:320 + 16 * r, :].astype(F32)

    def body(i, _):
        k = i // 8
        t = lax.rem(i, 8)
        base = 8 * hf + t + PADR
        total = jnp.sum(dws[k, 0, 0:9, :], axis=0, keepdims=True)
        depth[k, t, 0:32, :] = (xscr[k, base, PADC:PADC + 32, :] * total).astype(BF)
        for s in range(1, 4):
            n = WIN[s]
            parts = []
            for j in range(3):
                c0 = PADC + BEG[s] + 3 * s * (j - 1)
                acc = None
                for a in range(3):
                    v = xscr[k, base + 3 * s * (a - 1), c0:c0 + n, :] * dws[k, s, 3 * a + j:3 * a + j + 1, :]
                    acc = v if acc is None else acc + v
                parts.append(acc)
            left, right = edge_masks(s, col, cp)
            out = parts[1] + jnp.where(left, parts[0], 0.0) + jnp.where(right, parts[2], 0.0)
            depth[k, t, SOFF[s]:SOFF[s] + n, :] = out.astype(BF)
        return 0

    lax.fori_loop(0, 32, body, 0)


def product_kernel(sc, off, wid, depth, wfull, x0, x1, x2, x3, keep, send, pscr):
    mz, mc = sc[3], sc[4]
    for s in range(4):
        n = WIN[s]
        acc = None
        for k in range(0, 4, 2):
            lhs = jnp.concatenate(
                [depth[k + d, :, SOFF[s]:SOFF[s] + n, :].reshape(8 * n, 128) for d in range(2)], axis=1)
            rhs = jnp.concatenate([wfull[k, s], wfull[k + 1, s]], axis=0)
            v = dotf(lhs, rhs)
            acc = v if acc is None else acc + v
        pscr[:, SOFF[s]:SOFF[s] + n, :] = acc.reshape(8, n, 256)
    for zr in range(2):
        zz = 2 * jnp.bitwise_xor(mz, zr)
        for r in range(2):
            keep[zr, r] = pscr[4 * mc + zz + r]
            for b in range(2):
                at = 768 * zr + 384 * b + 192 * r
                send[at:at + 192, :] = pscr[4 * (1 - mc) + zz + r, :, 128 * b:128 * b + 128].astype(BF)
        for k, x in enumerate((x0, x1, x2, x3)):
            at = 1536 + 64 * zr + 16 * k
            send[at:at + 16, :] = x[528 + 32 * zr:544 + 32 * zr, :]


def add_kernel(keep, rcore, x0, x1, x2, x3, out):
    for r in range(2):
        for b in range(2):
            at = 384 * b + 192 * r
            v = keep[1, r, :, 128 * b:128 * b + 128] + rcore[768 + at:960 + at, :].astype(F32)
            out[at:at + 192, :] = v.astype(BF)
    for k, x in enumerate((x0, x1, x2, x3)):
        out[768 + 32 * k:784 + 32 * k, :] = x[544:560, :]
        out[784 + 32 * k:800 + 32 * k, :] = rcore[1600 + 16 * k:1616 + 16 * k, :]


def middle_kernel(sc, off, wid, keep, rcore, rzl, own, ownz, ownc, ownzc, f0, f1, f2, f3, labels,
                  zout, res0, gkeep, gsend, pjs, upscr, gscr):
    q, zh, mz, mc = sc[1], sc[2], sc[3], sc[4]
    fs = (f0, f1, f2, f3)
    for k, zr, cr, blk in blocks(sc):
        rows = pl.ds(pl.multiple_of(16 * blk, 16), 16)
        for r in range(4):
            s = back(q, r)
            base = 48 * (4 * k + r)
            for b in range(3):
                at = base + 16 * b
                pjs[s, rows, 128 * b:128 * b + 128] = ((own, ownz), (ownc, ownzc))[cr][zr][at:at + 16, :]
        if zr == 0:
            u = fs[k][512:528, :] if cr == 0 else rcore[1536 + 16 * k:1552 + 16 * k, :]
        else:
            u = rzl[768 + 32 * k + 16 * cr:784 + 32 * k + 16 * cr, :]
        upscr[rows, :] = u.astype(F32)
    frame, cp = zh // 2, lax.rem(zh, 2)
    w = lax.broadcasted_iota(jnp.int32, (64, 128), 1)
    v = lax.broadcasted_iota(jnp.int32, (64, 128), 0)
    hot = jnp.bitwise_and(w - off[frame], 127) == jnp.bitwise_and(2 * (v - 16) + cp, 127)
    cols = []
    for r in range(2):
        row = 2 * (8 * sc[0] + 4 * mc + 2 * mz + r) + sc[6]
        lrow = labels[frame, pl.ds(row, 1), :]
        cols.append(jnp.sum(jnp.where(hot & (lrow != VOID), 1.0, 0.0), axis=1, keepdims=True))
    lab = jnp.concatenate(cols, axis=0)

    lane = lax.broadcasted_iota(jnp.int32, (8, 128), 1)
    sums = []
    for r in range(2):
        got = [rcore[384 * b + 192 * r:384 * b + 192 * r + 192, :].astype(F32)
               + rzl[384 * b + 192 * r:384 * b + 192 * r + 192, :].astype(F32) for b in range(2)]
        sums.append(keep[0, r] + jnp.concatenate(got, axis=1))
    pre_now = jnp.stack(sums)
    pres, acts = [], []
    z = dotf(jnp.where((lane >= 3) & (lane < 6), 1.0, 0.0).astype(BF), pjs[0, :, 256:384], ((1,), (1,)))[0:1, :]
    for s in range(4):
        n, v0 = WIN[s], BEG[s] + 16
        bias = dotf(jnp.where(lane < 3, 1.0, 0.0).astype(BF), pjs[s, :, 256:384], ((1,), (1,)))[0:1, :]
        body = pre_now[:, SOFF[s]:SOFF[s] + n, :]
        if n < 64:
            body = jnp.concatenate(
                [jnp.zeros((2, v0, 256), F32), body, jnp.zeros((2, 64 - n - v0, 256), F32)], axis=1)
        pre = body.reshape(128, 256) + bias
        act = (pre * jax.nn.sigmoid(pre)).astype(BF)
        z = z + dotf(act, pjs[s, :, 0:256])
        pres.append(pre)
        acts.append(act)
    sig = jax.nn.sigmoid(z)
    res_t = jnp.transpose(z * sig)
    up = jnp.transpose(upscr[...])
    og = (up * (sig * (1.0 + z * (1.0 - sig))) * lab).astype(BF)
    ones = jnp.full((128, 128), 1.0, BF)
    half = lax.broadcasted_iota(jnp.int32, (256, 128), 1) < 64
    pbg = dotf(og, ones, ((0,), (0,)))
    for s in range(4):
        n, v0 = WIN[s], BEG[s] + 16
        pre = pres[s]
        sg = jax.nn.sigmoid(pre)
        ag = dotf(og, pjs[s, :, 0:256], ((1,), (1,)))
        pgs = (ag * (sg * (1.0 + pre * (1.0 - sg)))).astype(BF)
        for b in range(2):
            for r in range(2):
                at = 384 * b + 192 * r + SOFF[s]
                zout[at:at + n, :] = pgs[64 * r + v0:64 * r + v0 + n, 128 * b:128 * b + 128]
        gscr[s, :, 0:256] = dotf(acts[s], og, ((0,), (0,)))
        gscr[s, :, 256:384] = jnp.where(half, dotf(pgs, ones, ((0,), (0,))), pbg)
    upscr[...] = res_t
    for k, zr, cr, blk in blocks(sc):
        rows = pl.ds(pl.multiple_of(16 * blk, 16), 16)
        at = 64 * cr + 16 * k
        if zr == 0:
            res0[at:at + 16, :] = upscr[rows, :].astype(BF)
        else:
            zout[768 + at:784 + at, :] = upscr[rows, :].astype(BF)
        for r in range(4):
            g = gscr[lax.rem(q + r, 4), rows, :]
            if cr == 0:
                gkeep[zr, r, k] = g
            else:
                gsend[zr, r, k] = g.astype(BF)


def weight_kernel(sc, off, wid, depth, zout, zin, cin, res0, g0, g1, g2, g3, pgs, gbuf):
    mz, mc = sc[3], sc[4]
    for zr in range(2):
        for cr in range(2):
            t0 = 4 * jnp.bitwise_xor(mc, cr) + 2 * jnp.bitwise_xor(mz, zr)
            src, at0 = (cin, 768 * zr) if cr == 1 else ((zout, 0) if zr == 0 else (zin, 0))
            for r in range(2):
                for b in range(2):
                    at = at0 + 384 * b + 192 * r
                    pgs[t0 + r, :, 128 * b:128 * b + 128] = src[at:at + 192, :]
    for s in range(4):
        n = WIN[s]
        pg = pgs[:, SOFF[s]:SOFF[s] + n, :].reshape(8 * n, 256)
        for k in range(4):
            dep = depth[k, :, SOFF[s]:SOFF[s] + n, :].reshape(8 * n, 128)
            g = dotf(dep, pg, ((0,), (0,)))
            gbuf[s, 256 * k:256 * k + 128, :] = g[:, 0:128].astype(BF)
            gbuf[s, 256 * k + 128:256 * k + 256, :] = g[:, 128:256].astype(BF)
    for r, g in enumerate((g0, g1, g2, g3)):
        g[0:1024, :] = gbuf[lax.rem(sc[1] + r, 4)]
        for b, (src, at) in enumerate(((res0, 0), (cin, 1536), (zin, 768), (cin, 1600))):
            g[1024 + 64 * b:1088 + 64 * b, :] = src[at:at + 64, :]


def backward_kernel(sc, off, wid, x0, x1, x2, x3, wfull, dws, pgs, gpr,
                    o0, o1, o2, o3, xscr, dgs, yscr, dwa):
    hf, q, f, cp = sc[0], sc[1], sc[2] // 2, lax.rem(sc[2], 2)
    col = off[f]
    fill_x((x0, x1, x2, x3), xscr)
    for s in range(4):
        n = WIN[s]
        pg = pgs[:, SOFF[s]:SOFF[s] + n, :].reshape(8 * n, 256)
        for k in range(4):
            dgk = dotf(pg, wfull[k, s], ((1,), (1,))).astype(BF).astype(F32)
            dgs[k, :, SOFF[s]:SOFF[s] + n, :] = dgk.reshape(8, n, 128)
    yscr[...] = jnp.zeros(yscr.shape, F32)
    dwa[...] = jnp.zeros(dwa.shape, F32)

    def fold(v):
        n = v.shape[0]
        acc = v[0:8]
        for c in range(8, n, 8):
            acc = acc + v[c:c + 8]
        return acc

    def body(i, _):
        k = i // 8
        t = lax.rem(i, 8)
        base = 8 * hf + t + PADR
        d0 = dgs[k, t, 0:32, :]
        total = jnp.sum(dws[k, 0, 0:9, :], axis=0, keepdims=True)
        dwa[k, 0, 0:8, :] += fold(d0 * xscr[k, base, PADC:PADC + 32, :])
        yscr[k, t + PADR] += d0 * total
        for s in range(1, 4):
            n = WIN[s]
            left, right = edge_masks(s, col, cp)
            d = dgs[k, t, SOFF[s]:SOFF[s] + n, :]
            ds3 = (jnp.where(left, d, 0.0), d, jnp.where(right, d, 0.0))
            for a in range(3):
                for j in range(3):
                    c0 = PADC + BEG[s] + 3 * s * (j - 1)
                    v = fold(ds3[j] * xscr[k, base + 3 * s * (a - 1), c0:c0 + n, :])
                    tap = 9 * s + 3 * a + j - 8
                    dwa[k, tap, 0:8, :] += v
            acc = [None, None, None]
            for j in range(3):
                c1 = -BEG[s] - 3 * s * (j - 1)
                dv = ds3[j][c1:c1 + 32]
                for a in range(3):
                    v = dv * dws[k, s, 3 * a + j:3 * a + j + 1, :]
                    acc[a] = v if acc[a] is None else acc[a] + v
            for a in range(3):
                yscr[k, t + PADR + 3 * s * (a - 1)] += acc[a]
        return 0

    lax.fori_loop(0, 32, body, 0)
    for k in range(4):
        for s in range(4):
            rows = []
            for tap in range(9):
                src = 0 if s == 0 else 9 * s + tap - 8
                rows.append(jnp.sum(dwa[k, src], axis=0, keepdims=True))
            rows.append(jnp.zeros((7, 128), F32))
            dws_sum = jnp.concatenate(rows, axis=0)
            dwa[k, 28 + 2 * s] = dws_sum[0:8]
            dwa[k, 29 + 2 * s] = dws_sum[8:16]
    for r, o in enumerate((o0, o1, o2, o3)):
        dest = lax.rem(q + r, 4)
        for k in range(4):
            for b in range(4):
                at = 128 * k + 32 * b
                o[at:at + 32, :] = yscr[k, PADR - 8 * hf + 4 * dest + b].astype(BF)
            o[512 + 16 * k:528 + 16 * k, :] = jnp.concatenate(
                [dwa[k, 28 + 2 * dest], dwa[k, 29 + 2 * dest]], axis=0).astype(BF)
            for b in range(3):
                at = 576 + 48 * k + 16 * b
                o[at:at + 16, :] = gpr[r, k, :, 128 * b:128 * b + 128].astype(BF)


def combine_kernel(v0, v1, v2, v3, o0, o1, o2, o3):
    for k, o in enumerate((o0, o1, o2, o3)):
        ys = slice(128 * k, 128 * k + 128)
        o[0:128, :] = (v0[ys, :].astype(F32) + v2[ys, :].astype(F32)).astype(BF)
        o[128:256, :] = (v1[ys, :].astype(F32) + v3[ys, :].astype(F32)).astype(BF)
        for at, src, n in ((256, 512 + 16 * k, 16), (272, 576 + 48 * k, 48)):
            tot = v0[src:src + n, :].astype(F32)
            for v in (v1, v2, v3):
                tot = tot + v[src:src + n, :].astype(F32)
            o[at:at + n, :] = tot.astype(BF)


def gather_kernel(g0, g1, g2, g3, own, o0, o1, o2, o3):
    gs = (g0, g1, g2, g3)
    for k, o in enumerate((o0, o1, o2, o3)):
        tot = g0[256 * k:256 * k + 256, :].astype(F32)
        for g in gs[1:]:
            tot = tot + g[256 * k:256 * k + 256, :].astype(F32)
        if k == 0:
            own[...] = tot
        o[0:256, :] = tot.astype(BF)
        for r, g in enumerate(gs):
            for b in range(4):
                at = 256 + 64 * r + 16 * b
                o[at:at + 16, :] = g[1024 + 64 * b + 16 * k:1040 + 64 * b + 16 * k, :]


def sum_kernel(z0, z1, z2, z3, gown, h1, h2, h3, own, ownb):
    tot = gown[...]
    for h in (h1, h2, h3):
        tot = tot + h[0:256, :].astype(F32)
    own[0:256, :] = tot
    ownb[0:256, :] = tot.astype(BF)
    tot = z0[256:320, :].astype(F32)
    for z in (z1, z2, z3):
        tot = tot + z[256:320, :].astype(F32)
    own[256:320, :] = tot
    ownb[256:320, :] = tot.astype(BF)


def restore_kernel(sc, off, wid, z0, z1, z2, z3, h0, h1, h2, h3, out, asp, zs, rs, ascr):
    q, zh, mz, mc, rp = sc[1], sc[2], sc[3], sc[4], sc[6]
    for k, (z, h) in enumerate(((z0, h0), (z1, h1), (z2, h2), (z3, h3))):
        src = lax.rem(zh + k, 4)
        zs[src] = z[...]
        rs[src] = h[256:512, :]
    for f in range(2):
        w = lax.broadcasted_iota(jnp.int32, (128, 64), 0)
        x = lax.broadcasted_iota(jnp.int32, (128, 64), 1)
        tgt = 2 * jnp.bitwise_and(x, 31) + jnp.right_shift(x, 5)
        hot = jnp.where((jnp.bitwise_and(w - off[f], 127) == tgt) & (tgt < wid[f]), 1.0, 0.0).astype(BF)
        for rho in range(2):
            par = jnp.bitwise_xor(rp, rho)
            for b in range(4):
                at = 128 * rho + 32 * b
                both = jnp.concatenate([zs[2 * f, at:at + 32, :], zs[2 * f + 1, at:at + 32, :]], axis=0)
                out[f, 2 * b + par] = dotf(hot, both).astype(BF)
        for r in range(4):
            qs = back(q, r)
            for zr in range(2):
                for cr in range(2):
                    t0 = 8 * (qs // 2) + 4 * jnp.bitwise_xor(mc, cr) + 2 * jnp.bitwise_xor(mz, zr)
                    at = 64 * r + 32 * zr + 16 * cr
                    for e in range(2):
                        h = 2 * (t0 + e) + lax.rem(qs, 2)
                        ascr[h] = jnp.concatenate(
                            [rs[2 * f, at:at + 16, 64 * e:64 * e + 64],
                             rs[2 * f + 1, at:at + 16, 64 * e:64 * e + 64]], axis=1)
        asp[f] = dotf(ascr[...].reshape(512, 128), perm_matrix(off[f], True)).astype(BF).reshape(32, 16, 128)


def final_kernel(own, d1, d2, d3, dw, pw, pwb, proj, pb, *, scaling):
    tot = (own[...] + d1[...].astype(F32) + d2[...].astype(F32) + d3[...].astype(F32)) * scaling
    pw[0, :, 0:128] = tot[0:128]
    pw[0, :, 128:256] = tot[128:256]
    for t in range(9):
        dw[t] = tot[256 + t:257 + t]
    proj[0, :, 0:128] = tot[272:288]
    proj[0, :, 128:256] = tot[288:304]
    ext = tot[304:320]
    i = lax.broadcasted_iota(jnp.int32, (16, 16), 0)
    j = lax.broadcasted_iota(jnp.int32, (16, 16), 1)
    for o, lane in ((pwb, 0), (pb, 64)):
        col = jnp.broadcast_to(ext[:, lane:lane + 1], (16, 16))
        o[...] = jnp.sum(jnp.where(i == j, col, 0.0), axis=0, keepdims=True)


def call(kernel, scalars, args, outs, scratch=(), in_specs=None, us=1):
    whole = pl.BlockSpec(memory_space=pltpu.VMEM)
    specs = in_specs if in_specs is not None else [whole] * len(args)
    return pl.pallas_call(
        kernel,
        grid_spec=pltpu.PrefetchScalarGridSpec(
            num_scalar_prefetch=len(scalars), grid=(1,), in_specs=specs,
            out_specs=[pl.BlockSpec(o[0], lambda *a, n=len(o[0]): (0,) * n) for o in outs],
            scratch_shapes=[pltpu.VMEM(s, d) for s, d in scratch]),
        out_shape=[jax.ShapeDtypeStruct(s, d) for s, d in outs],
        compiler_params=pltpu.CompilerParams(vmem_limit_bytes=VM),
        cost_estimate=pl.CostEstimate(flops=us * 10 ** 9, bytes_accessed=us * 3 * 10 ** 6, transcendentals=0),
    )(*scalars, *args)


def local(feats, offsets, widths, labels, dw_kernel, pw_weight, pw_bias, proj, proj_bias, upstream):
    q = lax.axis_index("section")
    hf, rp = q // 2, q % 2
    scal = jnp.stack([hf, q, lax.axis_index("zh"), lax.axis_index("zl"), lax.axis_index("core"),
                      lax.axis_index("dp"), rp]).astype(jnp.int32)
    sc = (scal, offsets, widths)
    scaling = 1.0 / math.sqrt(8192.0 * lax.axis_size("dp"))

    (blk,) = call(pack_kernel, sc, [pw_weight, dw_kernel, proj, pw_bias, proj_bias[None]], [((128, 128), BF)])
    wb = gather_rel(blk, "section")

    upx = upstream.reshape(16, 2, 2, 8, 2, 128)
    upx = lax.dynamic_slice(upx, (0, 0, hf, 0, rp, 0), (16, 2, 1, 8, 1, 128)).reshape(16, 2, 8, 128)
    upx = upx.transpose(1, 2, 0, 3)
    xs = call(
        select_kernel, sc, [feats.reshape(2, 16, 2, 128, 128), upx], [((576, 128), BF)] * 4,
        scratch=[((4, 8, 16, 64), F32)], us=5,
        in_specs=[pl.BlockSpec((2, 16, 1, 128, 128), lambda i, sc, off, wid: (0, 0, sc[6], 0, 0)),
                  pl.BlockSpec((2, 8, 16, 128), lambda i, *a: (0, 0, 0, 0))])

    wb, xs = lax.optimization_barrier((wb, xs))
    (wown,) = call(branch_kernel, sc, wb, [((368, 128), BF)])
    wown, xs = lax.optimization_barrier((wown, xs))
    wz = gather_rel(wown, "zh")
    quart = jnp.concatenate([a[0:304] for a in wz], axis=0)
    xs = [xs[0]] + [shift(xs[k], "zh", k) for k in range(1, 4)]
    quarters = gather_rel(quart, "dp")
    own, wfull = call(proj_kernel, sc, quarters, [((768, 128), BF), ((4, 4, 128, 256), BF)])
    xs, own, wfull = lax.optimization_barrier((xs, own, wfull))
    depth, dws = call(
        depth_kernel, sc, [*xs, *wz], [((4, 8, NCOL, 128), BF), ((4, 4, 16, 128), F32)],
        scratch=[((4, 34, 96, 128), F32)], us=6)
    ownz = shift(own, "zl", 1)
    ownc = shift(own, "core", 1)
    ownzc = shift(ownz, "core", 1)
    keep, send = call(
        product_kernel, sc, [depth, wfull, *xs], [((2, 2, NCOL, 256), F32), ((1664, 128), BF)],
        scratch=[((8, NCOL, 256), F32)], us=4)
    rcore = shift(send, "core", 1)
    (zsend,) = call(add_kernel, (), [keep, rcore, *xs], [((896, 128), BF)])
    rzl = shift(zsend, "zl", 1)
    zout, res0, gkeep, gsend = call(
        middle_kernel, sc, [keep, rcore, rzl, own, ownz, ownc, ownzc, *xs, labels],
        [((896, 128), BF), ((128, 128), BF), ((2, 4, 4, 16, 384), F32), ((2, 4, 4, 16, 384), BF)],
        scratch=[((4, 256, 384), BF), ((256, 128), F32), ((4, 256, 384), F32)], us=5)

    zin = shift(zout, "zl", 1)
    cin = shift(jnp.concatenate([zout[0:768], zin[0:768], res0[64:128], zin[832:896]], axis=0), "core", 1)
    gz = gkeep + shift(gsend, "core", 1).astype(F32)

    *gs, pgs = call(
        weight_kernel, sc, [depth, zout, zin, cin, res0],
        [((1280, 128), BF)] * 4 + [((8, NCOL, 256), BF)], scratch=[((4, 1024, 128), BF)], us=4)
    gs = [gs[0]] + [shift(gs[k], "section", k) for k in range(1, 4)]
    gz, pgs = lax.optimization_barrier((gz, pgs))
    gpr = gz[0] + shift(gz[1].astype(BF), "zl", 1).astype(F32)
    vs = call(
        backward_kernel, sc, [*xs, wfull, dws, pgs, gpr], [((768, 128), BF)] * 4,
        scratch=[((4, 34, 96, 128), F32), ((4, 8, NCOL, 128), F32), ((4, 26, 32, 128), F32), ((4, 36, 8, 128), F32)],
        us=10)
    vs = [vs[0]] + [shift(vs[k], "section", k) for k in range(1, 4)]

    gown, *hs = call(gather_kernel, (), gs, [((256, 128), F32)] + [((512, 128), BF)] * 4)
    hs = [hs[0]] + [shift(hs[k], "zh", -k) for k in range(1, 4)]

    zs = call(combine_kernel, (), vs, [((320, 128), BF)] * 4)
    zs = [zs[0]] + [shift(zs[k], "zh", -k) for k in range(1, 4)]
    own, ownb = call(sum_kernel, (), [*zs, gown, *hs[1:]], [((320, 128), F32), ((320, 128), BF)])
    input_grad, asp = call(
        restore_kernel, sc, [*zs, *hs],
        [((2, 8, 128, 128), BF), ((2, 32, 16, 128), BF)],
        scratch=[((4, 320, 128), BF), ((4, 256, 128), BF), ((32, 16, 128), BF)], us=3)
    outs = call(
        functools.partial(final_kernel, scaling=scaling), (), [own] + [shift(ownb, "dp", k) for k in range(1, 4)],
        [((9, 1, 128), F32), ((1, 128, 256), F32), ((1, 16), F32), ((1, 16, 256), F32), ((1, 16), F32)])
    grad_dw, grad_pw, grad_pwb, grad_proj, grad_pb = outs
    aspp = asp.transpose(2, 0, 1, 3)
    return (aspp, input_grad, grad_dw.reshape(1, 9, 128), grad_pw, grad_pwb, grad_proj, grad_pb[0])


def solution(mesh):
    fine = Mesh(mesh.devices.reshape(4, 4, 4, 2, 2), ("section", "dp", "zh", "zl", "core"))
    chan = ("zh", "zl", "core")
    in_specs = (
        P("dp", None, None, chan),
        P("dp"),
        P("dp"),
        P("dp", None, None),
        P("section", None, chan),
        P("section", chan, None),
        P("section", chan),
        P("section", chan, None),
        P(chan),
        P(chan, "dp", None, None),
    )
    out_specs = (
        P(chan, "dp", None, None),
        P("dp", "section", None, chan),
        P("section", None, chan),
        P("section", chan, None),
        P("section", chan),
        P("section", chan, None),
        P(chan),
    )
    return jax.shard_map(local, mesh=fine, in_specs=in_specs, out_specs=out_specs, check_vma=False)
```

```python
import functools
import math

import jax
import jax.numpy as jnp
from jax import lax
from jax.experimental import pallas as pl
from jax.experimental.pallas import tpu as pltpu
from jax.sharding import Mesh, PartitionSpec as P

RATE = 6
VOID = 19
BF = jnp.bfloat16
F32 = jnp.float32

WIN = (32, 48, 48, 64)
BEG = (0, -8, -8, -16)
SOFF = (0, 32, 80, 128)
NCOL = 192
PADC = 32
PADR = 9
VM = 56 * 1024 * 1024


def shift(x, axis, k):
    n = lax.axis_size(axis)
    return lax.ppermute(x, axis, [(i, (i + k) % n) for i in range(n)])


def gather_rel(x, axis):
    n = lax.axis_size(axis)
    return [x] + [shift(x, axis, k) for k in range(1, n)]


def dotf(a, b, dims=((1,), (0,))):
    return lax.dot_general(a, b, (dims, ((), ())), preferred_element_type=F32)


def back(a, k):
    return lax.rem(a - k + 4, 4)


def blocks(sc):
    for k in range(4):
        for zr in range(2):
            for cr in range(2):
                yield k, zr, cr, 4 * back(sc[2], k) + 2 * jnp.bitwise_xor(sc[3], zr) + jnp.bitwise_xor(sc[4], cr)


def perm_matrix(off, transpose=False):
    w = lax.broadcasted_iota(jnp.int32, (128, 128), 1 if transpose else 0)
    x = lax.broadcasted_iota(jnp.int32, (128, 128), 0 if transpose else 1)
    col = 2 * (jnp.bitwise_and(x, 63) - 16) + jnp.right_shift(x, 6)
    return jnp.where(jnp.bitwise_and(w - off, 127) == jnp.bitwise_and(col, 127), 1.0, 0.0).astype(BF)


def pack_kernel(sc, off, wid, pw, dw, proj, pwb, pb, out):
    rows = pl.ds(pl.multiple_of(32 * sc[5], 32), 32)
    out[0:32, :] = pw[0, rows, 0:128]
    out[32:64, :] = pw[0, rows, 128:256]
    out[80:96, :] = proj[0, :, 0:128]
    out[96:112, :] = proj[0, :, 128:256]
    i = lax.broadcasted_iota(jnp.int32, (16, 16), 0)
    j = lax.broadcasted_iota(jnp.int32, (16, 16), 1)
    lane = lax.broadcasted_iota(jnp.int32, (16, 128), 1)
    ext = jnp.zeros((16, 128), F32)
    for n, b in enumerate((pwb, pb)):
        rest = jnp.sum(jnp.where(i == j, b[...], 0.0), axis=1, keepdims=True)
        for piece in range(3):
            part = rest.astype(BF).astype(F32)
            ext = ext + jnp.where(lane == 3 * n + piece, part, 0.0)
            rest = rest - part
    out[112:128, :] = ext.astype(BF)
    taps = jnp.concatenate([dw[0].astype(F32), jnp.zeros((7, 128), F32)], axis=0)
    out[64:80, :] = taps.astype(BF)


def branch_kernel(sc, off, wid, b0, b1, b2, b3, out):
    for r, b in enumerate((b0, b1, b2, b3)):
        out[64 * r:64 * r + 64, :] = b[0:64, :]
        out[304 + 16 * r:320 + 16 * r, :] = b[64:80, :]

        @pl.when(sc[5] == r)
        def _(b=b):
            out[256:304, :] = b[80:128, :]


def proj_kernel(sc, off, wid, q0, q1, q2, q3, own, wfull):
    for j, qj in enumerate((q0, q1, q2, q3)):
        d = back(sc[5], j)
        lanes = pl.ds(pl.multiple_of(32 * d, 32), 32)
        for k in range(4):
            for r in range(4):
                s = back(sc[1], r)
                for b in range(2):
                    at = 304 * k + 64 * r + 32 * b
                    wfull[k, s, lanes, 128 * b:128 * b + 128] = qj[at:at + 32, :]
            at = 304 * k + 256
            own[pl.ds(pl.multiple_of(192 * k + 48 * d, 16), 48), :] = qj[at:at + 48, :]


def select_kernel(sc, off, wid, x, up, o0, o1, o2, o3, uscr):
    for f in range(2):
        res = dotf(up[f].reshape(128, 128), perm_matrix(off[f]))
        for p in range(2):
            uscr[2 * f + p] = res[:, 64 * p:64 * p + 64].reshape(8, 16, 64)
    for k, o in enumerate((o0, o1, o2, o3)):
        dest = lax.rem(sc[2] + k, 4)
        f, p = dest // 2, lax.rem(dest, 2)
        w = lax.broadcasted_iota(jnp.int32, (32, 128), 1)
        tgt = 2 * lax.broadcasted_iota(jnp.int32, (32, 128), 0) + p
        hot = jnp.where((jnp.bitwise_and(w - off[f], 127) == tgt) & (tgt < wid[f]), 1.0, 0.0).astype(BF)

        def body(t, _, o=o, hot=hot, f=f):
            o[pl.ds(pl.multiple_of(32 * t, 32), 32), :] = dotf(hot, x[f, t, 0]).astype(BF)
            return 0

        lax.fori_loop(0, 16, body, 0, unroll=8)
        for zr in range(2):
            for cr in range(2):
                t0 = 4 * jnp.bitwise_xor(sc[4], cr) + 2 * jnp.bitwise_xor(sc[3], zr)
                row = 512 + 32 * zr + 16 * cr
                o[row:row + 16, :] = jnp.concatenate([uscr[dest, t0], uscr[dest, t0 + 1]], axis=1).astype(BF)


def edge_masks(s, off, cp):
    n = WIN[s]
    u = lax.broadcasted_iota(jnp.int32, (n, 128), 0) + BEG[s]
    w = jnp.bitwise_and(off + 2 * u + cp, 127)
    return w >= RATE * s, w < 128 - RATE * s


def fill_x(xs, xscr):
    xscr[...] = jnp.zeros(xscr.shape, F32)
    for k in range(4):
        def body(t, _, k=k):
            xscr[k, PADR + t, PADC:PADC + 32, :] = xs[k][pl.ds(pl.multiple_of(32 * t, 32), 32), :].astype(F32)
            return 0
        lax.fori_loop(0, 16, body, 0, unroll=4)


def depth_kernel(sc, off, wid, x0, x1, x2, x3, a0, a1, a2, a3, depth, dws, xscr):
    hf, f, cp = sc[0], sc[2] // 2, lax.rem(sc[2], 2)
    col = off[f]
    fill_x((x0, x1, x2, x3), xscr)
    for k, a in enumerate((a0, a1, a2, a3)):
        for r in range(4):
            dws[k, back(sc[1], r)] = a[304 + 16 * r:320 + 16 * r, :].astype(F32)

    def body(i, _):
        k = i // 8
        t = lax.rem(i, 8)
        base = 8 * hf + t + PADR
        total = jnp.sum(dws[k, 0, 0:9, :], axis=0, keepdims=True)
        depth[k, t, 0:32, :] = (xscr[k, base, PADC:PADC + 32, :] * total).astype(BF)
        for s in range(1, 4):
            n = WIN[s]
            parts = []
            for j in range(3):
                c0 = PADC + BEG[s] + 3 * s * (j - 1)
                acc = None
                for a in range(3):
                    v = xscr[k, base + 3 * s * (a - 1), c0:c0 + n, :] * dws[k, s, 3 * a + j:3 * a + j + 1, :]
                    acc = v if acc is None else acc + v
                parts.append(acc)
            left, right = edge_masks(s, col, cp)
            out = parts[1] + jnp.where(left, parts[0], 0.0) + jnp.where(right, parts[2], 0.0)
            depth[k, t, SOFF[s]:SOFF[s] + n, :] = out.astype(BF)
        return 0

    lax.fori_loop(0, 32, body, 0)


def product_kernel(sc, off, wid, depth, wfull, x0, x1, x2, x3, keep, send, pscr):
    mz, mc = sc[3], sc[4]
    for s in range(4):
        n = WIN[s]
        acc = None
        for k in range(0, 4, 2):
            lhs = jnp.concatenate(
                [depth[k + d, :, SOFF[s]:SOFF[s] + n, :].reshape(8 * n, 128) for d in range(2)], axis=1)
            rhs = jnp.concatenate([wfull[k, s], wfull[k + 1, s]], axis=0)
            v = dotf(lhs, rhs)
            acc = v if acc is None else acc + v
        pscr[:, SOFF[s]:SOFF[s] + n, :] = acc.reshape(8, n, 256)
    for zr in range(2):
        zz = 2 * jnp.bitwise_xor(mz, zr)
        for r in range(2):
            keep[zr, r] = pscr[4 * mc + zz + r]
            for b in range(2):
                at = 768 * zr + 384 * b + 192 * r
                send[at:at + 192, :] = pscr[4 * (1 - mc) + zz + r, :, 128 * b:128 * b + 128].astype(BF)
        for k, x in enumerate((x0, x1, x2, x3)):
            at = 1536 + 64 * zr + 16 * k
            send[at:at + 16, :] = x[528 + 32 * zr:544 + 32 * zr, :]


def add_kernel(keep, rcore, x0, x1, x2, x3, out):
    for r in range(2):
        for b in range(2):
            at = 384 * b + 192 * r
            v = keep[1, r, :, 128 * b:128 * b + 128] + rcore[768 + at:960 + at, :].astype(F32)
            out[at:at + 192, :] = v.astype(BF)
    for k, x in enumerate((x0, x1, x2, x3)):
        out[768 + 32 * k:784 + 32 * k, :] = x[544:560, :]
        out[784 + 32 * k:800 + 32 * k, :] = rcore[1600 + 16 * k:1616 + 16 * k, :]


def middle_kernel(sc, off, wid, keep, rcore, rzl, own, ownz, ownc, ownzc, f0, f1, f2, f3, labels,
                  zout, res0, gkeep, gsend, pjs, upscr, gscr):
    q, zh, mz, mc = sc[1], sc[2], sc[3], sc[4]
    fs = (f0, f1, f2, f3)
    for k, zr, cr, blk in blocks(sc):
        rows = pl.ds(pl.multiple_of(16 * blk, 16), 16)
        for r in range(4):
            s = back(q, r)
            base = 48 * (4 * k + r)
            for b in range(3):
                at = base + 16 * b
                pjs[s, rows, 128 * b:128 * b + 128] = ((own, ownz), (ownc, ownzc))[cr][zr][at:at + 16, :]
        if zr == 0:
            u = fs[k][512:528, :] if cr == 0 else rcore[1536 + 16 * k:1552 + 16 * k, :]
        else:
            u = rzl[768 + 32 * k + 16 * cr:784 + 32 * k + 16 * cr, :]
        upscr[rows, :] = u.astype(F32)
    frame, cp = zh // 2, lax.rem(zh, 2)
    w = lax.broadcasted_iota(jnp.int32, (64, 128), 1)
    v = lax.broadcasted_iota(jnp.int32, (64, 128), 0)
    hot = jnp.bitwise_and(w - off[frame], 127) == jnp.bitwise_and(2 * (v - 16) + cp, 127)
    cols = []
    for r in range(2):
        row = 2 * (8 * sc[0] + 4 * mc + 2 * mz + r) + sc[6]
        lrow = labels[frame, pl.ds(row, 1), :]
        cols.append(jnp.sum(jnp.where(hot & (lrow != VOID), 1.0, 0.0), axis=1, keepdims=True))
    lab = jnp.concatenate(cols, axis=0)

    lane = lax.broadcasted_iota(jnp.int32, (8, 128), 1)
    sums = []
    for r in range(2):
        got = [rcore[384 * b + 192 * r:384 * b + 192 * r + 192, :].astype(F32)
               + rzl[384 * b + 192 * r:384 * b + 192 * r + 192, :].astype(F32) for b in range(2)]
        sums.append(keep[0, r] + jnp.concatenate(got, axis=1))
    pre_now = jnp.stack(sums)
    pres, acts = [], []
    z = dotf(jnp.where((lane >= 3) & (lane < 6), 1.0, 0.0).astype(BF), pjs[0, :, 256:384], ((1,), (1,)))[0:1, :]
    for s in range(4):
        n, v0 = WIN[s], BEG[s] + 16
        bias = dotf(jnp.where(lane < 3, 1.0, 0.0).astype(BF), pjs[s, :, 256:384], ((1,), (1,)))[0:1, :]
        body = pre_now[:, SOFF[s]:SOFF[s] + n, :]
        if n < 64:
            body = jnp.concatenate(
                [jnp.zeros((2, v0, 256), F32), body, jnp.zeros((2, 64 - n - v0, 256), F32)], axis=1)
        pre = body.reshape(128, 256) + bias
        act = (pre * jax.nn.sigmoid(pre)).astype(BF)
        z = z + dotf(act, pjs[s, :, 0:256])
        pres.append(pre)
        acts.append(act)
    sig = jax.nn.sigmoid(z)
    res_t = jnp.transpose(z * sig)
    up = jnp.transpose(upscr[...])
    og = (up * (sig * (1.0 + z * (1.0 - sig))) * lab).astype(BF)
    ones = jnp.full((128, 128), 1.0, BF)
    half = lax.broadcasted_iota(jnp.int32, (256, 128), 1) < 64
    pbg = dotf(og, ones, ((0,), (0,)))
    for s in range(4):
        n, v0 = WIN[s], BEG[s] + 16
        pre = pres[s]
        sg = jax.nn.sigmoid(pre)
        ag = dotf(og, pjs[s, :, 0:256], ((1,), (1,)))
        pgs = (ag * (sg * (1.0 + pre * (1.0 - sg)))).astype(BF)
        for b in range(2):
            for r in range(2):
                at = 384 * b + 192 * r + SOFF[s]
                zout[at:at + n, :] = pgs[64 * r + v0:64 * r + v0 + n, 128 * b:128 * b + 128]
        gscr[s, :, 0:256] = dotf(acts[s], og, ((0,), (0,)))
        gscr[s, :, 256:384] = jnp.where(half, dotf(pgs, ones, ((0,), (0,))), pbg)
    upscr[...] = res_t
    for k, zr, cr, blk in blocks(sc):
        rows = pl.ds(pl.multiple_of(16 * blk, 16), 16)
        at = 64 * cr + 16 * k
        if zr == 0:
            res0[at:at + 16, :] = upscr[rows, :].astype(BF)
        else:
            zout[768 + at:784 + at, :] = upscr[rows, :].astype(BF)
        for r in range(4):
            g = gscr[lax.rem(q + r, 4), rows, :]
            if cr == 0:
                gkeep[zr, r, k] = g
            else:
                gsend[zr, r, k] = g.astype(BF)


def weight_kernel(sc, off, wid, depth, zout, zin, cin, res0, g0, g1, g2, g3, pgs, gbuf):
    mz, mc = sc[3], sc[4]
    for zr in range(2):
        for cr in range(2):
            t0 = 4 * jnp.bitwise_xor(mc, cr) + 2 * jnp.bitwise_xor(mz, zr)
            src, at0 = (cin, 768 * zr) if cr == 1 else ((zout, 0) if zr == 0 else (zin, 0))
            for r in range(2):
                for b in range(2):
                    at = at0 + 384 * b + 192 * r
                    pgs[t0 + r, :, 128 * b:128 * b + 128] = src[at:at + 192, :]
    for s in range(4):
        n = WIN[s]
        pg = pgs[:, SOFF[s]:SOFF[s] + n, :].reshape(8 * n, 256)
        for k in range(4):
            dep = depth[k, :, SOFF[s]:SOFF[s] + n, :].reshape(8 * n, 128)
            g = dotf(dep, pg, ((0,), (0,)))
            gbuf[s, 256 * k:256 * k + 128, :] = g[:, 0:128].astype(BF)
            gbuf[s, 256 * k + 128:256 * k + 256, :] = g[:, 128:256].astype(BF)
    for r, g in enumerate((g0, g1, g2, g3)):
        g[0:1024, :] = gbuf[lax.rem(sc[1] + r, 4)]
        for b, (src, at) in enumerate(((res0, 0), (cin, 1536), (zin, 768), (cin, 1600))):
            g[1024 + 64 * b:1088 + 64 * b, :] = src[at:at + 64, :]


def backward_kernel(sc, off, wid, x0, x1, x2, x3, wfull, dws, pgs, gpr,
                    o0, o1, o2, o3, xscr, dgs, yscr, dwa):
    hf, q, f, cp = sc[0], sc[1], sc[2] // 2, lax.rem(sc[2], 2)
    col = off[f]
    fill_x((x0, x1, x2, x3), xscr)
    for s in range(4):
        n = WIN[s]
        pg = pgs[:, SOFF[s]:SOFF[s] + n, :].reshape(8 * n, 256)
        for k in range(4):
            dgk = dotf(pg, wfull[k, s], ((1,), (1,))).astype(BF).astype(F32)
            dgs[k, :, SOFF[s]:SOFF[s] + n, :] = dgk.reshape(8, n, 128)
    yscr[...] = jnp.zeros(yscr.shape, F32)
    dwa[...] = jnp.zeros(dwa.shape, F32)

    def fold(v):
        n = v.shape[0]
        acc = v[0:8]
        for c in range(8, n, 8):
            acc = acc + v[c:c + 8]
        return acc

    def body(i, _):
        k = i // 8
        t = lax.rem(i, 8)
        base = 8 * hf + t + PADR
        d0 = dgs[k, t, 0:32, :]
        total = jnp.sum(dws[k, 0, 0:9, :], axis=0, keepdims=True)
        dwa[k, 0, 0:8, :] += fold(d0 * xscr[k, base, PADC:PADC + 32, :])
        yscr[k, t + PADR] += d0 * total
        for s in range(1, 4):
            n = WIN[s]
            left, right = edge_masks(s, col, cp)
            d = dgs[k, t, SOFF[s]:SOFF[s] + n, :]
            ds3 = (jnp.where(left, d, 0.0), d, jnp.where(right, d, 0.0))
            for a in range(3):
                for j in range(3):
                    c0 = PADC + BEG[s] + 3 * s * (j - 1)
                    v = fold(ds3[j] * xscr[k, base + 3 * s * (a - 1), c0:c0 + n, :])
                    tap = 9 * s + 3 * a + j - 8
                    dwa[k, tap, 0:8, :] += v
            acc = [None, None, None]
            for j in range(3):
                c1 = -BEG[s] - 3 * s * (j - 1)
                dv = ds3[j][c1:c1 + 32]
                for a in range(3):
                    v = dv * dws[k, s, 3 * a + j:3 * a + j + 1, :]
                    acc[a] = v if acc[a] is None else acc[a] + v
            for a in range(3):
                yscr[k, t + PADR + 3 * s * (a - 1)] += acc[a]
        return 0

    lax.fori_loop(0, 32, body, 0)
    for k in range(4):
        for s in range(4):
            rows = []
            for tap in range(9):
                src = 0 if s == 0 else 9 * s + tap - 8
                rows.append(jnp.sum(dwa[k, src], axis=0, keepdims=True))
            rows.append(jnp.zeros((7, 128), F32))
            dws_sum = jnp.concatenate(rows, axis=0)
            dwa[k, 28 + 2 * s] = dws_sum[0:8]
            dwa[k, 29 + 2 * s] = dws_sum[8:16]
    for r, o in enumerate((o0, o1, o2, o3)):
        dest = lax.rem(q + r, 4)
        for k in range(4):
            for b in range(4):
                at = 128 * k + 32 * b
                o[at:at + 32, :] = yscr[k, PADR - 8 * hf + 4 * dest + b].astype(BF)
            o[512 + 16 * k:528 + 16 * k, :] = jnp.concatenate(
                [dwa[k, 28 + 2 * dest], dwa[k, 29 + 2 * dest]], axis=0).astype(BF)
            for b in range(3):
                at = 576 + 48 * k + 16 * b
                o[at:at + 16, :] = gpr[r, k, :, 128 * b:128 * b + 128].astype(BF)


def combine_kernel(v0, v1, v2, v3, o0, o1, o2, o3):
    for k, o in enumerate((o0, o1, o2, o3)):
        ys = slice(128 * k, 128 * k + 128)
        o[0:128, :] = (v0[ys, :].astype(F32) + v2[ys, :].astype(F32)).astype(BF)
        o[128:256, :] = (v1[ys, :].astype(F32) + v3[ys, :].astype(F32)).astype(BF)
        for at, src, n in ((256, 512 + 16 * k, 16), (272, 576 + 48 * k, 48)):
            tot = v0[src:src + n, :].astype(F32)
            for v in (v1, v2, v3):
                tot = tot + v[src:src + n, :].astype(F32)
            o[at:at + n, :] = tot.astype(BF)


def gather_kernel(g0, g1, g2, g3, own, o0, o1, o2, o3):
    gs = (g0, g1, g2, g3)
    for k, o in enumerate((o0, o1, o2, o3)):
        tot = g0[256 * k:256 * k + 256, :].astype(F32)
        for g in gs[1:]:
            tot = tot + g[256 * k:256 * k + 256, :].astype(F32)
        if k == 0:
            own[...] = tot
        o[0:256, :] = tot.astype(BF)
        for r, g in enumerate(gs):
            for b in range(4):
                at = 256 + 64 * r + 16 * b
                o[at:at + 16, :] = g[1024 + 64 * b + 16 * k:1040 + 64 * b + 16 * k, :]


def sum_kernel(z0, z1, z2, z3, gown, h1, h2, h3, own, ownb):
    tot = gown[...]
    for h in (h1, h2, h3):
        tot = tot + h[0:256, :].astype(F32)
    own[0:256, :] = tot
    ownb[0:256, :] = tot.astype(BF)
    tot = z0[256:320, :].astype(F32)
    for z in (z1, z2, z3):
        tot = tot + z[256:320, :].astype(F32)
    own[256:320, :] = tot
    ownb[256:320, :] = tot.astype(BF)


def restore_kernel(sc, off, wid, z0, z1, z2, z3, h0, h1, h2, h3, out, asp, zs, rs, ascr):
    q, zh, mz, mc, rp = sc[1], sc[2], sc[3], sc[4], sc[6]
    for k, (z, h) in enumerate(((z0, h0), (z1, h1), (z2, h2), (z3, h3))):
        src = lax.rem(zh + k, 4)
        zs[src] = z[...]
        rs[src] = h[256:512, :]
    for f in range(2):
        w = lax.broadcasted_iota(jnp.int32, (128, 64), 0)
        x = lax.broadcasted_iota(jnp.int32, (128, 64), 1)
        tgt = 2 * jnp.bitwise_and(x, 31) + jnp.right_shift(x, 5)
        hot = jnp.where((jnp.bitwise_and(w - off[f], 127) == tgt) & (tgt < wid[f]), 1.0, 0.0).astype(BF)
        for rho in range(2):
            par = jnp.bitwise_xor(rp, rho)
            for b in range(4):
                at = 128 * rho + 32 * b
                both = jnp.concatenate([zs[2 * f, at:at + 32, :], zs[2 * f + 1, at:at + 32, :]], axis=0)
                out[f, 2 * b + par] = dotf(hot, both).astype(BF)
        for r in range(4):
            qs = back(q, r)
            for zr in range(2):
                for cr in range(2):
                    t0 = 8 * (qs // 2) + 4 * jnp.bitwise_xor(mc, cr) + 2 * jnp.bitwise_xor(mz, zr)
                    at = 64 * r + 32 * zr + 16 * cr
                    for e in range(2):
                        h = 2 * (t0 + e) + lax.rem(qs, 2)
                        ascr[f, h] = jnp.concatenate(
                            [rs[2 * f, at:at + 16, 64 * e:64 * e + 64],
                             rs[2 * f + 1, at:at + 16, 64 * e:64 * e + 64]], axis=1)
        asp[f] = dotf(ascr[f].reshape(512, 128), perm_matrix(off[f], True)).astype(BF).reshape(32, 16, 128)


def final_kernel(own, d1, d2, d3, dw, pw, pwb, proj, pb, *, scaling):
    tot = (own[...] + d1[...].astype(F32) + d2[...].astype(F32) + d3[...].astype(F32)) * scaling
    pw[0, :, 0:128] = tot[0:128]
    pw[0, :, 128:256] = tot[128:256]
    for t in range(9):
        dw[t] = tot[256 + t:257 + t]
    proj[0, :, 0:128] = tot[272:288]
    proj[0, :, 128:256] = tot[288:304]
    ext = tot[304:320]
    i = lax.broadcasted_iota(jnp.int32, (16, 16), 0)
    j = lax.broadcasted_iota(jnp.int32, (16, 16), 1)
    for o, lane in ((pwb, 0), (pb, 64)):
        col = jnp.broadcast_to(ext[:, lane:lane + 1], (16, 16))
        o[...] = jnp.sum(jnp.where(i == j, col, 0.0), axis=0, keepdims=True)


def call(kernel, scalars, args, outs, scratch=(), in_specs=None, us=1):
    whole = pl.BlockSpec(memory_space=pltpu.VMEM)
    specs = in_specs if in_specs is not None else [whole] * len(args)
    return pl.pallas_call(
        kernel,
        grid_spec=pltpu.PrefetchScalarGridSpec(
            num_scalar_prefetch=len(scalars), grid=(1,), in_specs=specs,
            out_specs=[pl.BlockSpec(o[0], lambda *a, n=len(o[0]): (0,) * n) for o in outs],
            scratch_shapes=[pltpu.VMEM(s, d) for s, d in scratch]),
        out_shape=[jax.ShapeDtypeStruct(s, d) for s, d in outs],
        compiler_params=pltpu.CompilerParams(vmem_limit_bytes=VM),
        cost_estimate=pl.CostEstimate(flops=us * 10 ** 9, bytes_accessed=us * 3 * 10 ** 6, transcendentals=0),
    )(*scalars, *args)


def local(feats, offsets, widths, labels, dw_kernel, pw_weight, pw_bias, proj, proj_bias, upstream):
    q = lax.axis_index("section")
    hf, rp = q // 2, q % 2
    scal = jnp.stack([hf, q, lax.axis_index("zh"), lax.axis_index("zl"), lax.axis_index("core"),
                      lax.axis_index("dp"), rp]).astype(jnp.int32)
    sc = (scal, offsets, widths)
    scaling = 1.0 / math.sqrt(8192.0 * lax.axis_size("dp"))

    (blk,) = call(pack_kernel, sc, [pw_weight, dw_kernel, proj, pw_bias, proj_bias[None]], [((128, 128), BF)])
    wb = gather_rel(blk, "section")

    upx = upstream.reshape(16, 2, 2, 8, 2, 128)
    upx = lax.dynamic_slice(upx, (0, 0, hf, 0, rp, 0), (16, 2, 1, 8, 1, 128)).reshape(16, 2, 8, 128)
    upx = upx.transpose(1, 2, 0, 3)
    xs = call(
        select_kernel, sc, [feats.reshape(2, 16, 2, 128, 128), upx], [((576, 128), BF)] * 4,
        scratch=[((4, 8, 16, 64), F32)], us=5,
        in_specs=[pl.BlockSpec((2, 16, 1, 128, 128), lambda i, sc, off, wid: (0, 0, sc[6], 0, 0)),
                  pl.BlockSpec((2, 8, 16, 128), lambda i, *a: (0, 0, 0, 0))])

    wb, xs = lax.optimization_barrier((wb, xs))
    (wown,) = call(branch_kernel, sc, wb, [((368, 128), BF)])
    wown, xs = lax.optimization_barrier((wown, xs))
    wz = gather_rel(wown, "zh")
    quart = jnp.concatenate([a[0:304] for a in wz], axis=0)
    xs = [xs[0]] + [shift(xs[k], "zh", k) for k in range(1, 4)]
    quarters = gather_rel(quart, "dp")
    own, wfull = call(proj_kernel, sc, quarters, [((768, 128), BF), ((4, 4, 128, 256), BF)])
    xs, own, wfull = lax.optimization_barrier((xs, own, wfull))
    depth, dws = call(
        depth_kernel, sc, [*xs, *wz], [((4, 8, NCOL, 128), BF), ((4, 4, 16, 128), F32)],
        scratch=[((4, 34, 96, 128), F32)], us=6)
    ownz = shift(own, "zl", 1)
    ownc = shift(own, "core", 1)
    ownzc = shift(ownz, "core", 1)
    keep, send = call(
        product_kernel, sc, [depth, wfull, *xs], [((2, 2, NCOL, 256), F32), ((1664, 128), BF)],
        scratch=[((8, NCOL, 256), F32)], us=4)
    rcore = shift(send, "core", 1)
    (zsend,) = call(add_kernel, (), [keep, rcore, *xs], [((896, 128), BF)])
    rzl = shift(zsend, "zl", 1)
    zout, res0, gkeep, gsend = call(
        middle_kernel, sc, [keep, rcore, rzl, own, ownz, ownc, ownzc, *xs, labels],
        [((896, 128), BF), ((128, 128), BF), ((2, 4, 4, 16, 384), F32), ((2, 4, 4, 16, 384), BF)],
        scratch=[((4, 256, 384), BF), ((256, 128), F32), ((4, 256, 384), F32)], us=5)

    zin = shift(zout, "zl", 1)
    cin = shift(jnp.concatenate([zout[0:768], zin[0:768], res0[64:128], zin[832:896]], axis=0), "core", 1)
    gz = gkeep + shift(gsend, "core", 1).astype(F32)

    *gs, pgs = call(
        weight_kernel, sc, [depth, zout, zin, cin, res0],
        [((1280, 128), BF)] * 4 + [((8, NCOL, 256), BF)], scratch=[((4, 1024, 128), BF)], us=4)
    gs = [gs[0]] + [shift(gs[k], "section", k) for k in range(1, 4)]
    gz, pgs = lax.optimization_barrier((gz, pgs))
    gpr = gz[0] + shift(gz[1].astype(BF), "zl", 1).astype(F32)
    vs = call(
        backward_kernel, sc, [*xs, wfull, dws, pgs, gpr], [((768, 128), BF)] * 4,
        scratch=[((4, 34, 96, 128), F32), ((4, 8, NCOL, 128), F32), ((4, 26, 32, 128), F32), ((4, 36, 8, 128), F32)],
        us=10)
    vs = [vs[0]] + [shift(vs[k], "section", k) for k in range(1, 4)]

    gown, *hs = call(gather_kernel, (), gs, [((256, 128), F32)] + [((512, 128), BF)] * 4)
    hs = [hs[0]] + [shift(hs[k], "zh", -k) for k in range(1, 4)]

    zs = call(combine_kernel, (), vs, [((320, 128), BF)] * 4)
    zs = [zs[0]] + [shift(zs[k], "zh", -k) for k in range(1, 4)]
    own, ownb = call(sum_kernel, (), [*zs, gown, *hs[1:]], [((320, 128), F32), ((320, 128), BF)])
    input_grad, asp = call(
        restore_kernel, sc, [*zs, *hs],
        [((2, 8, 128, 128), BF), ((2, 32, 16, 128), BF)],
        scratch=[((4, 320, 128), BF), ((4, 256, 128), BF), ((2, 32, 16, 128), BF)], us=3)
    outs = call(
        functools.partial(final_kernel, scaling=scaling), (), [own] + [shift(ownb, "dp", k) for k in range(1, 4)],
        [((9, 1, 128), F32), ((1, 128, 256), F32), ((1, 16), F32), ((1, 16, 256), F32), ((1, 16), F32)])
    grad_dw, grad_pw, grad_pwb, grad_proj, grad_pb = outs
    aspp = asp.transpose(2, 0, 1, 3)
    return (aspp, input_grad, grad_dw.reshape(1, 9, 128), grad_pw, grad_pwb, grad_proj, grad_pb[0])


def solution(mesh):
    fine = Mesh(mesh.devices.reshape(4, 4, 4, 2, 2), ("section", "dp", "zh", "zl", "core"))
    chan = ("zh", "zl", "core")
    in_specs = (
        P("dp", None, None, chan),
        P("dp"),
        P("dp"),
        P("dp", None, None),
        P("section", None, chan),
        P("section", chan, None),
        P("section", chan),
        P("section", chan, None),
        P(chan),
        P(chan, "dp", None, None),
    )
    out_specs = (
        P(chan, "dp", None, None),
        P("dp", "section", None, chan),
        P("section", None, chan),
        P("section", chan, None),
        P("section", chan),
        P("section", chan, None),
        P(chan),
    )
    return jax.shard_map(local, mesh=fine, in_specs=in_specs, out_specs=out_specs, check_vma=False)
```

```python
import functools
import math

import jax
import jax.numpy as jnp
from jax import lax
from jax.experimental import pallas as pl
from jax.experimental.pallas import tpu as pltpu
from jax.sharding import Mesh, PartitionSpec as P

RATE = 6
VOID = 19
BF = jnp.bfloat16
F32 = jnp.float32

WIN = (32, 48, 48, 64)
BEG = (0, -8, -8, -16)
SOFF = (0, 32, 80, 128)
NCOL = 192
PADC = 32
PADR = 9
VM = 56 * 1024 * 1024


def shift(x, axis, k):
    n = lax.axis_size(axis)
    return lax.ppermute(x, axis, [(i, (i + k) % n) for i in range(n)])


def gather_rel(x, axis):
    n = lax.axis_size(axis)
    return [x] + [shift(x, axis, k) for k in range(1, n)]


def dotf(a, b, dims=((1,), (0,))):
    return lax.dot_general(a, b, (dims, ((), ())), preferred_element_type=F32)


def back(a, k):
    return lax.rem(a - k + 4, 4)


def blocks(sc):
    for k in range(4):
        for zr in range(2):
            for cr in range(2):
                yield k, zr, cr, 4 * back(sc[2], k) + 2 * jnp.bitwise_xor(sc[3], zr) + jnp.bitwise_xor(sc[4], cr)


def perm_matrix(off, transpose=False):
    w = lax.broadcasted_iota(jnp.int32, (128, 128), 1 if transpose else 0)
    x = lax.broadcasted_iota(jnp.int32, (128, 128), 0 if transpose else 1)
    col = 2 * (jnp.bitwise_and(x, 63) - 16) + jnp.right_shift(x, 6)
    return jnp.where(jnp.bitwise_and(w - off, 127) == jnp.bitwise_and(col, 127), 1.0, 0.0).astype(BF)


def pack_kernel(sc, off, wid, pw, dw, proj, pwb, pb, out):
    rows = pl.ds(pl.multiple_of(32 * sc[5], 32), 32)
    out[0:32, :] = pw[0, rows, 0:128]
    out[32:64, :] = pw[0, rows, 128:256]
    out[80:96, :] = proj[0, :, 0:128]
    out[96:112, :] = proj[0, :, 128:256]
    i = lax.broadcasted_iota(jnp.int32, (16, 16), 0)
    j = lax.broadcasted_iota(jnp.int32, (16, 16), 1)
    lane = lax.broadcasted_iota(jnp.int32, (16, 128), 1)
    ext = jnp.zeros((16, 128), F32)
    for n, b in enumerate((pwb, pb)):
        rest = jnp.sum(jnp.where(i == j, b[...], 0.0), axis=1, keepdims=True)
        for piece in range(3):
            part = rest.astype(BF).astype(F32)
            ext = ext + jnp.where(lane == 3 * n + piece, part, 0.0)
            rest = rest - part
    out[112:128, :] = ext.astype(BF)
    taps = jnp.concatenate([dw[0].astype(F32), jnp.zeros((7, 128), F32)], axis=0)
    out[64:80, :] = taps.astype(BF)


def branch_kernel(sc, off, wid, b0, b1, b2, b3, out):
    for r, b in enumerate((b0, b1, b2, b3)):
        out[64 * r:64 * r + 64, :] = b[0:64, :]
        out[304 + 16 * r:320 + 16 * r, :] = b[64:80, :]

        @pl.when(sc[5] == r)
        def _(b=b):
            out[256:304, :] = b[80:128, :]


def proj_kernel(sc, off, wid, q0, q1, q2, q3, own, wfull):
    for j, qj in enumerate((q0, q1, q2, q3)):
        d = back(sc[5], j)
        lanes = pl.ds(pl.multiple_of(32 * d, 32), 32)
        for k in range(4):
            for r in range(4):
                s = back(sc[1], r)
                for b in range(2):
                    at = 304 * k + 64 * r + 32 * b
                    wfull[k, s, lanes, 128 * b:128 * b + 128] = qj[at:at + 32, :]
            at = 304 * k + 256
            own[pl.ds(pl.multiple_of(192 * k + 48 * d, 16), 48), :] = qj[at:at + 48, :]


def select_kernel(sc, off, wid, x, up, o0, o1, o2, o3, uscr):
    for f in range(2):
        res = dotf(up[f].reshape(128, 128), perm_matrix(off[f]))
        for p in range(2):
            uscr[2 * f + p] = res[:, 64 * p:64 * p + 64].reshape(8, 16, 64)
    for k, o in enumerate((o0, o1, o2, o3)):
        dest = lax.rem(sc[2] + k, 4)
        f, p = dest // 2, lax.rem(dest, 2)
        w = lax.broadcasted_iota(jnp.int32, (32, 128), 1)
        tgt = 2 * lax.broadcasted_iota(jnp.int32, (32, 128), 0) + p
        hot = jnp.where((jnp.bitwise_and(w - off[f], 127) == tgt) & (tgt < wid[f]), 1.0, 0.0).astype(BF)

        def body(t, _, o=o, hot=hot, f=f):
            o[pl.ds(pl.multiple_of(32 * t, 32), 32), :] = dotf(hot, x[f, t, 0]).astype(BF)
            return 0

        lax.fori_loop(0, 16, body, 0, unroll=8)
        for zr in range(2):
            for cr in range(2):
                t0 = 4 * jnp.bitwise_xor(sc[4], cr) + 2 * jnp.bitwise_xor(sc[3], zr)
                row = 512 + 32 * zr + 16 * cr
                o[row:row + 16, :] = jnp.concatenate([uscr[dest, t0], uscr[dest, t0 + 1]], axis=1).astype(BF)


def edge_masks(s, off, cp):
    n = WIN[s]
    u = lax.broadcasted_iota(jnp.int32, (n, 128), 0) + BEG[s]
    w = jnp.bitwise_and(off + 2 * u + cp, 127)
    return w >= RATE * s, w < 128 - RATE * s


def fill_x(xs, xscr):
    xscr[...] = jnp.zeros(xscr.shape, F32)
    for k in range(4):
        def body(t, _, k=k):
            xscr[k, PADR + t, PADC:PADC + 32, :] = xs[k][pl.ds(pl.multiple_of(32 * t, 32), 32), :].astype(F32)
            return 0
        lax.fori_loop(0, 16, body, 0, unroll=4)


def depth_kernel(sc, off, wid, x0, x1, x2, x3, a0, a1, a2, a3, depth, dws, xscr):
    hf, f, cp = sc[0], sc[2] // 2, lax.rem(sc[2], 2)
    col = off[f]
    fill_x((x0, x1, x2, x3), xscr)
    for k, a in enumerate((a0, a1, a2, a3)):
        for r in range(4):
            dws[k, back(sc[1], r)] = a[304 + 16 * r:320 + 16 * r, :].astype(F32)

    def body(i, _):
        k = i // 8
        t = lax.rem(i, 8)
        base = 8 * hf + t + PADR
        total = jnp.sum(dws[k, 0, 0:9, :], axis=0, keepdims=True)
        depth[k, t, 0:32, :] = (xscr[k, base, PADC:PADC + 32, :] * total).astype(BF)
        for s in range(1, 4):
            n = WIN[s]
            parts = []
            for j in range(3):
                c0 = PADC + BEG[s] + 3 * s * (j - 1)
                acc = None
                for a in range(3):
                    v = xscr[k, base + 3 * s * (a - 1), c0:c0 + n, :] * dws[k, s, 3 * a + j:3 * a + j + 1, :]
                    acc = v if acc is None else acc + v
                parts.append(acc)
            left, right = edge_masks(s, col, cp)
            out = parts[1] + jnp.where(left, parts[0], 0.0) + jnp.where(right, parts[2], 0.0)
            depth[k, t, SOFF[s]:SOFF[s] + n, :] = out.astype(BF)
        return 0

    lax.fori_loop(0, 32, body, 0)


def product_kernel(sc, off, wid, depth, wfull, x0, x1, x2, x3, keep0, keep1, send, ups, pscr):
    mz, mc = sc[3], sc[4]
    for s in range(4):
        n = WIN[s]
        acc = None
        for k in range(0, 4, 2):
            lhs = jnp.concatenate(
                [depth[k + d, :, SOFF[s]:SOFF[s] + n, :].reshape(8 * n, 128) for d in range(2)], axis=1)
            rhs = jnp.concatenate([wfull[k, s], wfull[k + 1, s]], axis=0)
            v = dotf(lhs, rhs)
            acc = v if acc is None else acc + v
        pscr[:, SOFF[s]:SOFF[s] + n, :] = acc.reshape(8, n, 256)
    for zr in range(2):
        zz = 2 * jnp.bitwise_xor(mz, zr)
        for r in range(2):
            (keep0, keep1)[zr][r] = pscr[4 * mc + zz + r]
            for b in range(2):
                at = 768 * zr + 384 * b + 192 * r
                send[at:at + 192, :] = pscr[4 * (1 - mc) + zz + r, :, 128 * b:128 * b + 128].astype(BF)
        for k, x in enumerate((x0, x1, x2, x3)):
            at = 1536 + 64 * zr + 16 * k
            send[at:at + 16, :] = x[528 + 32 * zr:544 + 32 * zr, :]
            ups[64 * zr + 16 * k:64 * zr + 16 * k + 16, :] = x[512 + 32 * zr:528 + 32 * zr, :]


def add_kernel(keep1, rcore, ups, out):
    for r in range(2):
        for b in range(2):
            at = 384 * b + 192 * r
            v = keep1[r, :, 128 * b:128 * b + 128] + rcore[768 + at:960 + at, :].astype(F32)
            out[at:at + 192, :] = v.astype(BF)
    for k in range(4):
        out[768 + 32 * k:784 + 32 * k, :] = ups[64 + 16 * k:80 + 16 * k, :]
        out[784 + 32 * k:800 + 32 * k, :] = rcore[1600 + 16 * k:1616 + 16 * k, :]


def middle_kernel(sc, off, wid, keep0, rcore, rzl, own, ownz, ownc, ownzc, ups, labels,
                  zout, res0, gkeep, gsend, pjs, upscr, gscr):
    q, zh, mz, mc = sc[1], sc[2], sc[3], sc[4]
    for k, zr, cr, blk in blocks(sc):
        rows = pl.ds(pl.multiple_of(16 * blk, 16), 16)
        for r in range(4):
            s = back(q, r)
            base = 48 * (4 * k + r)
            for b in range(3):
                at = base + 16 * b
                pjs[s, rows, 128 * b:128 * b + 128] = ((own, ownz), (ownc, ownzc))[cr][zr][at:at + 16, :]
        if zr == 0:
            u = ups[16 * k:16 * k + 16, :] if cr == 0 else rcore[1536 + 16 * k:1552 + 16 * k, :]
        else:
            u = rzl[768 + 32 * k + 16 * cr:784 + 32 * k + 16 * cr, :]
        upscr[rows, :] = u.astype(F32)
    frame, cp = zh // 2, lax.rem(zh, 2)
    w = lax.broadcasted_iota(jnp.int32, (64, 128), 1)
    v = lax.broadcasted_iota(jnp.int32, (64, 128), 0)
    hot = jnp.bitwise_and(w - off[frame], 127) == jnp.bitwise_and(2 * (v - 16) + cp, 127)
    cols = []
    for r in range(2):
        row = 2 * (8 * sc[0] + 4 * mc + 2 * mz + r) + sc[6]
        lrow = labels[frame, pl.ds(row, 1), :]
        cols.append(jnp.sum(jnp.where(hot & (lrow != VOID), 1.0, 0.0), axis=1, keepdims=True))
    lab = jnp.concatenate(cols, axis=0)

    lane = lax.broadcasted_iota(jnp.int32, (8, 128), 1)
    sums = []
    for r in range(2):
        got = [rcore[384 * b + 192 * r:384 * b + 192 * r + 192, :].astype(F32)
               + rzl[384 * b + 192 * r:384 * b + 192 * r + 192, :].astype(F32) for b in range(2)]
        sums.append(keep0[r] + jnp.concatenate(got, axis=1))
    pre_now = jnp.stack(sums)
    pres, acts = [], []
    z = dotf(jnp.where((lane >= 3) & (lane < 6), 1.0, 0.0).astype(BF), pjs[0, :, 256:384], ((1,), (1,)))[0:1, :]
    for s in range(4):
        n, v0 = WIN[s], BEG[s] + 16
        bias = dotf(jnp.where(lane < 3, 1.0, 0.0).astype(BF), pjs[s, :, 256:384], ((1,), (1,)))[0:1, :]
        body = pre_now[:, SOFF[s]:SOFF[s] + n, :]
        if n < 64:
            body = jnp.concatenate(
                [jnp.zeros((2, v0, 256), F32), body, jnp.zeros((2, 64 - n - v0, 256), F32)], axis=1)
        pre = body.reshape(128, 256) + bias
        act = (pre * jax.nn.sigmoid(pre)).astype(BF)
        z = z + dotf(act, pjs[s, :, 0:256])
        pres.append(pre)
        acts.append(act)
    sig = jax.nn.sigmoid(z)
    res_t = jnp.transpose(z * sig)
    up = jnp.transpose(upscr[...])
    og = (up * (sig * (1.0 + z * (1.0 - sig))) * lab).astype(BF)
    ones = jnp.full((128, 128), 1.0, BF)
    half = lax.broadcasted_iota(jnp.int32, (256, 128), 1) < 64
    pbg = dotf(og, ones, ((0,), (0,)))
    for s in range(4):
        n, v0 = WIN[s], BEG[s] + 16
        pre = pres[s]
        sg = jax.nn.sigmoid(pre)
        ag = dotf(og, pjs[s, :, 0:256], ((1,), (1,)))
        pgs = (ag * (sg * (1.0 + pre * (1.0 - sg)))).astype(BF)
        for b in range(2):
            for r in range(2):
                at = 384 * b + 192 * r + SOFF[s]
                zout[at:at + n, :] = pgs[64 * r + v0:64 * r + v0 + n, 128 * b:128 * b + 128]
        gscr[s, :, 0:256] = dotf(acts[s], og, ((0,), (0,)))
        gscr[s, :, 256:384] = jnp.where(half, dotf(pgs, ones, ((0,), (0,))), pbg)
    upscr[...] = res_t
    for k, zr, cr, blk in blocks(sc):
        rows = pl.ds(pl.multiple_of(16 * blk, 16), 16)
        at = 64 * cr + 16 * k
        if zr == 0:
            res0[at:at + 16, :] = upscr[rows, :].astype(BF)
        else:
            zout[768 + at:784 + at, :] = upscr[rows, :].astype(BF)
        for r in range(4):
            g = gscr[lax.rem(q + r, 4), rows, :]
            if cr == 0:
                gkeep[zr, r, k] = g
            else:
                gsend[zr, r, k] = g.astype(BF)


def weight_kernel(sc, off, wid, depth, zout, zin, cin, res0, g0, g1, g2, g3, pgs, gbuf):
    mz, mc = sc[3], sc[4]
    for zr in range(2):
        for cr in range(2):
            t0 = 4 * jnp.bitwise_xor(mc, cr) + 2 * jnp.bitwise_xor(mz, zr)
            src, at0 = (cin, 768 * zr) if cr == 1 else ((zout, 0) if zr == 0 else (zin, 0))
            for r in range(2):
                for b in range(2):
                    at = at0 + 384 * b + 192 * r
                    pgs[t0 + r, :, 128 * b:128 * b + 128] = src[at:at + 192, :]
    for s in range(4):
        n = WIN[s]
        pg = pgs[:, SOFF[s]:SOFF[s] + n, :].reshape(8 * n, 256)
        for k in range(4):
            dep = depth[k, :, SOFF[s]:SOFF[s] + n, :].reshape(8 * n, 128)
            g = dotf(dep, pg, ((0,), (0,)))
            gbuf[s, 256 * k:256 * k + 128, :] = g[:, 0:128].astype(BF)
            gbuf[s, 256 * k + 128:256 * k + 256, :] = g[:, 128:256].astype(BF)
    for r, g in enumerate((g0, g1, g2, g3)):
        g[0:1024, :] = gbuf[lax.rem(sc[1] + r, 4)]
        for b, (src, at) in enumerate(((res0, 0), (cin, 1536), (zin, 768), (cin, 1600))):
            g[1024 + 64 * b:1088 + 64 * b, :] = src[at:at + 64, :]


def backward_kernel(sc, off, wid, x0, x1, x2, x3, wfull, dws, pgs, gpr,
                    o0, o1, o2, o3, xscr, dgs, yscr, dwa):
    hf, q, f, cp = sc[0], sc[1], sc[2] // 2, lax.rem(sc[2], 2)
    col = off[f]
    fill_x((x0, x1, x2, x3), xscr)
    for s in range(4):
        n = WIN[s]
        pg = pgs[:, SOFF[s]:SOFF[s] + n, :].reshape(8 * n, 256)
        for k in range(4):
            dgk = dotf(pg, wfull[k, s], ((1,), (1,))).astype(BF).astype(F32)
            dgs[k, :, SOFF[s]:SOFF[s] + n, :] = dgk.reshape(8, n, 128)
    yscr[...] = jnp.zeros(yscr.shape, F32)
    dwa[...] = jnp.zeros(dwa.shape, F32)

    def fold(v):
        n = v.shape[0]
        acc = v[0:8]
        for c in range(8, n, 8):
            acc = acc + v[c:c + 8]
        return acc

    def body(i, _):
        k = i // 8
        t = lax.rem(i, 8)
        base = 8 * hf + t + PADR
        d0 = dgs[k, t, 0:32, :]
        total = jnp.sum(dws[k, 0, 0:9, :], axis=0, keepdims=True)
        dwa[k, 0, 0:8, :] += fold(d0 * xscr[k, base, PADC:PADC + 32, :])
        yscr[k, t + PADR] += d0 * total
        for s in range(1, 4):
            n = WIN[s]
            left, right = edge_masks(s, col, cp)
            d = dgs[k, t, SOFF[s]:SOFF[s] + n, :]
            ds3 = (jnp.where(left, d, 0.0), d, jnp.where(right, d, 0.0))
            for a in range(3):
                for j in range(3):
                    c0 = PADC + BEG[s] + 3 * s * (j - 1)
                    v = fold(ds3[j] * xscr[k, base + 3 * s * (a - 1), c0:c0 + n, :])
                    tap = 9 * s + 3 * a + j - 8
                    dwa[k, tap, 0:8, :] += v
            acc = [None, None, None]
            for j in range(3):
                c1 = -BEG[s] - 3 * s * (j - 1)
                dv = ds3[j][c1:c1 + 32]
                for a in range(3):
                    v = dv * dws[k, s, 3 * a + j:3 * a + j + 1, :]
                    acc[a] = v if acc[a] is None else acc[a] + v
            for a in range(3):
                yscr[k, t + PADR + 3 * s * (a - 1)] += acc[a]
        return 0

    lax.fori_loop(0, 32, body, 0)
    for k in range(4):
        for s in range(4):
            rows = []
            for tap in range(9):
                src = 0 if s == 0 else 9 * s + tap - 8
                rows.append(jnp.sum(dwa[k, src], axis=0, keepdims=True))
            rows.append(jnp.zeros((7, 128), F32))
            dws_sum = jnp.concatenate(rows, axis=0)
            dwa[k, 28 + 2 * s] = dws_sum[0:8]
            dwa[k, 29 + 2 * s] = dws_sum[8:16]
    for r, o in enumerate((o0, o1, o2, o3)):
        dest = lax.rem(q + r, 4)
        for k in range(4):
            for b in range(4):
                at = 128 * k + 32 * b
                o[at:at + 32, :] = yscr[k, PADR - 8 * hf + 4 * dest + b].astype(BF)
            o[512 + 16 * k:528 + 16 * k, :] = jnp.concatenate(
                [dwa[k, 28 + 2 * dest], dwa[k, 29 + 2 * dest]], axis=0).astype(BF)
            for b in range(3):
                at = 576 + 48 * k + 16 * b
                o[at:at + 16, :] = gpr[r, k, :, 128 * b:128 * b + 128].astype(BF)


def combine_kernel(v0, v1, v2, v3, o0, o1, o2, o3):
    for k, o in enumerate((o0, o1, o2, o3)):
        ys = slice(128 * k, 128 * k + 128)
        o[0:128, :] = (v0[ys, :].astype(F32) + v2[ys, :].astype(F32)).astype(BF)
        o[128:256, :] = (v1[ys, :].astype(F32) + v3[ys, :].astype(F32)).astype(BF)
        for at, src, n in ((256, 512 + 16 * k, 16), (272, 576 + 48 * k, 48)):
            tot = v0[src:src + n, :].astype(F32)
            for v in (v1, v2, v3):
                tot = tot + v[src:src + n, :].astype(F32)
            o[at:at + n, :] = tot.astype(BF)


def gather_kernel(g0, g1, g2, g3, own, o0, o1, o2, o3):
    gs = (g0, g1, g2, g3)
    for k, o in enumerate((o0, o1, o2, o3)):
        tot = g0[256 * k:256 * k + 256, :].astype(F32)
        for g in gs[1:]:
            tot = tot + g[256 * k:256 * k + 256, :].astype(F32)
        if k == 0:
            own[...] = tot
        o[0:256, :] = tot.astype(BF)
        for r, g in enumerate(gs):
            for b in range(4):
                at = 256 + 64 * r + 16 * b
                o[at:at + 16, :] = g[1024 + 64 * b + 16 * k:1040 + 64 * b + 16 * k, :]


def sum_kernel(z0, z1, z2, z3, gown, h1, h2, h3, own, ownb):
    tot = gown[...]
    for h in (h1, h2, h3):
        tot = tot + h[0:256, :].astype(F32)
    own[0:256, :] = tot
    ownb[0:256, :] = tot.astype(BF)
    tot = z0[256:320, :].astype(F32)
    for z in (z1, z2, z3):
        tot = tot + z[256:320, :].astype(F32)
    own[256:320, :] = tot
    ownb[256:320, :] = tot.astype(BF)


def restore_kernel(sc, off, wid, z0, z1, z2, z3, h0, h1, h2, h3, out, asp, zs, rs, ascr):
    q, zh, mz, mc, rp = sc[1], sc[2], sc[3], sc[4], sc[6]
    for k, (z, h) in enumerate(((z0, h0), (z1, h1), (z2, h2), (z3, h3))):
        src = lax.rem(zh + k, 4)
        zs[src] = z[...]
        rs[src] = h[256:512, :]
    for f in range(2):
        w = lax.broadcasted_iota(jnp.int32, (128, 64), 0)
        x = lax.broadcasted_iota(jnp.int32, (128, 64), 1)
        tgt = 2 * jnp.bitwise_and(x, 31) + jnp.right_shift(x, 5)
        hot = jnp.where((jnp.bitwise_and(w - off[f], 127) == tgt) & (tgt < wid[f]), 1.0, 0.0).astype(BF)
        for rho in range(2):
            par = jnp.bitwise_xor(rp, rho)
            for b in range(4):
                at = 128 * rho + 32 * b
                both = jnp.concatenate([zs[2 * f, at:at + 32, :], zs[2 * f + 1, at:at + 32, :]], axis=0)
                out[f, 2 * b + par] = dotf(hot, both).astype(BF)
        for r in range(4):
            qs = back(q, r)
            for zr in range(2):
                for cr in range(2):
                    t0 = 8 * (qs // 2) + 4 * jnp.bitwise_xor(mc, cr) + 2 * jnp.bitwise_xor(mz, zr)
                    at = 64 * r + 32 * zr + 16 * cr
                    for e in range(2):
                        h = 2 * (t0 + e) + lax.rem(qs, 2)
                        ascr[f, h] = jnp.concatenate(
                            [rs[2 * f, at:at + 16, 64 * e:64 * e + 64],
                             rs[2 * f + 1, at:at + 16, 64 * e:64 * e + 64]], axis=1)
        asp[f] = dotf(ascr[f].reshape(512, 128), perm_matrix(off[f], True)).astype(BF).reshape(32, 16, 128)


def final_kernel(own, d1, d2, d3, dw, pw, pwb, proj, pb, *, scaling):
    tot = (own[...] + d1[...].astype(F32) + d2[...].astype(F32) + d3[...].astype(F32)) * scaling
    pw[0, :, 0:128] = tot[0:128]
    pw[0, :, 128:256] = tot[128:256]
    for t in range(9):
        dw[t] = tot[256 + t:257 + t]
    proj[0, :, 0:128] = tot[272:288]
    proj[0, :, 128:256] = tot[288:304]
    ext = tot[304:320]
    i = lax.broadcasted_iota(jnp.int32, (16, 16), 0)
    j = lax.broadcasted_iota(jnp.int32, (16, 16), 1)
    for o, lane in ((pwb, 0), (pb, 64)):
        col = jnp.broadcast_to(ext[:, lane:lane + 1], (16, 16))
        o[...] = jnp.sum(jnp.where(i == j, col, 0.0), axis=0, keepdims=True)


def call(kernel, scalars, args, outs, scratch=(), in_specs=None, us=1):
    whole = pl.BlockSpec(memory_space=pltpu.VMEM)
    specs = in_specs if in_specs is not None else [whole] * len(args)
    return pl.pallas_call(
        kernel,
        grid_spec=pltpu.PrefetchScalarGridSpec(
            num_scalar_prefetch=len(scalars), grid=(1,), in_specs=specs,
            out_specs=[pl.BlockSpec(o[0], lambda *a, n=len(o[0]): (0,) * n) for o in outs],
            scratch_shapes=[pltpu.VMEM(s, d) for s, d in scratch]),
        out_shape=[jax.ShapeDtypeStruct(s, d) for s, d in outs],
        compiler_params=pltpu.CompilerParams(vmem_limit_bytes=VM),
        cost_estimate=pl.CostEstimate(flops=us * 10 ** 9, bytes_accessed=us * 3 * 10 ** 6, transcendentals=0),
    )(*scalars, *args)


def local(feats, offsets, widths, labels, dw_kernel, pw_weight, pw_bias, proj, proj_bias, upstream):
    q = lax.axis_index("section")
    hf, rp = q // 2, q % 2
    scal = jnp.stack([hf, q, lax.axis_index("zh"), lax.axis_index("zl"), lax.axis_index("core"),
                      lax.axis_index("dp"), rp]).astype(jnp.int32)
    sc = (scal, offsets, widths)
    scaling = 1.0 / math.sqrt(8192.0 * lax.axis_size("dp"))

    (blk,) = call(pack_kernel, sc, [pw_weight, dw_kernel, proj, pw_bias, proj_bias[None]], [((128, 128), BF)])
    wb = gather_rel(blk, "section")

    upx = upstream.reshape(16, 2, 2, 8, 2, 128)
    upx = lax.dynamic_slice(upx, (0, 0, hf, 0, rp, 0), (16, 2, 1, 8, 1, 128)).reshape(16, 2, 8, 128)
    upx = upx.transpose(1, 2, 0, 3)
    xs = call(
        select_kernel, sc, [feats.reshape(2, 16, 2, 128, 128), upx], [((576, 128), BF)] * 4,
        scratch=[((4, 8, 16, 64), F32)], us=5,
        in_specs=[pl.BlockSpec((2, 16, 1, 128, 128), lambda i, sc, off, wid: (0, 0, sc[6], 0, 0)),
                  pl.BlockSpec((2, 8, 16, 128), lambda i, *a: (0, 0, 0, 0))])

    wb, xs = lax.optimization_barrier((wb, xs))
    (wown,) = call(branch_kernel, sc, wb, [((368, 128), BF)])
    wown, xs = lax.optimization_barrier((wown, xs))
    wz = gather_rel(wown, "zh")
    quart = jnp.concatenate([a[0:304] for a in wz], axis=0)
    xs = [xs[0]] + [shift(xs[k], "zh", k) for k in range(1, 4)]
    quarters = gather_rel(quart, "dp")
    own, wfull = call(proj_kernel, sc, quarters, [((768, 128), BF), ((4, 4, 128, 256), BF)])
    xs, own, wfull = lax.optimization_barrier((xs, own, wfull))
    depth, dws = call(
        depth_kernel, sc, [*xs, *wz], [((4, 8, NCOL, 128), BF), ((4, 4, 16, 128), F32)],
        scratch=[((4, 34, 96, 128), F32)], us=6)
    ownz = shift(own, "zl", 1)
    ownc = shift(own, "core", 1)
    ownzc = shift(ownz, "core", 1)
    keep0, keep1, send, ups = call(
        product_kernel, sc, [depth, wfull, *xs], [((2, NCOL, 256), F32), ((2, NCOL, 256), F32), ((1664, 128), BF), ((128, 128), BF)],
        scratch=[((8, NCOL, 256), F32)], us=4)
    rcore = shift(send, "core", 1)
    (zsend,) = call(add_kernel, (), [keep1, rcore, ups], [((896, 128), BF)])
    rzl = shift(zsend, "zl", 1)
    zout, res0, gkeep, gsend = call(
        middle_kernel, sc, [keep0, rcore, rzl, own, ownz, ownc, ownzc, ups, labels],
        [((896, 128), BF), ((128, 128), BF), ((2, 4, 4, 16, 384), F32), ((2, 4, 4, 16, 384), BF)],
        scratch=[((4, 256, 384), BF), ((256, 128), F32), ((4, 256, 384), F32)], us=5)

    zin = shift(zout, "zl", 1)
    cin = shift(jnp.concatenate([zout[0:768], zin[0:768], res0[64:128], zin[832:896]], axis=0), "core", 1)
    gz = gkeep + shift(gsend, "core", 1).astype(F32)

    *gs, pgs = call(
        weight_kernel, sc, [depth, zout, zin, cin, res0],
        [((1280, 128), BF)] * 4 + [((8, NCOL, 256), BF)], scratch=[((4, 1024, 128), BF)], us=4)
    gs = [gs[0]] + [shift(gs[k], "section", k) for k in range(1, 4)]
    gz, pgs = lax.optimization_barrier((gz, pgs))
    gpr = gz[0] + shift(gz[1].astype(BF), "zl", 1).astype(F32)
    vs = call(
        backward_kernel, sc, [*xs, wfull, dws, pgs, gpr], [((768, 128), BF)] * 4,
        scratch=[((4, 34, 96, 128), F32), ((4, 8, NCOL, 128), F32), ((4, 26, 32, 128), F32), ((4, 36, 8, 128), F32)],
        us=10)
    vs = [vs[0]] + [shift(vs[k], "section", k) for k in range(1, 4)]

    gown, *hs = call(gather_kernel, (), gs, [((256, 128), F32)] + [((512, 128), BF)] * 4)
    hs = [hs[0]] + [shift(hs[k], "zh", -k) for k in range(1, 4)]

    zs = call(combine_kernel, (), vs, [((320, 128), BF)] * 4)
    zs = [zs[0]] + [shift(zs[k], "zh", -k) for k in range(1, 4)]
    own, ownb = call(sum_kernel, (), [*zs, gown, *hs[1:]], [((320, 128), F32), ((320, 128), BF)])
    input_grad, asp = call(
        restore_kernel, sc, [*zs, *hs],
        [((2, 8, 128, 128), BF), ((2, 32, 16, 128), BF)],
        scratch=[((4, 320, 128), BF), ((4, 256, 128), BF), ((2, 32, 16, 128), BF)], us=3)
    outs = call(
        functools.partial(final_kernel, scaling=scaling), (), [own] + [shift(ownb, "dp", k) for k in range(1, 4)],
        [((9, 1, 128), F32), ((1, 128, 256), F32), ((1, 16), F32), ((1, 16, 256), F32), ((1, 16), F32)])
    grad_dw, grad_pw, grad_pwb, grad_proj, grad_pb = outs
    aspp = asp.transpose(2, 0, 1, 3)
    return (aspp, input_grad, grad_dw.reshape(1, 9, 128), grad_pw, grad_pwb, grad_proj, grad_pb[0])


def solution(mesh):
    fine = Mesh(mesh.devices.reshape(4, 4, 4, 2, 2), ("section", "dp", "zh", "zl", "core"))
    chan = ("zh", "zl", "core")
    in_specs = (
        P("dp", None, None, chan),
        P("dp"),
        P("dp"),
        P("dp", None, None),
        P("section", None, chan),
        P("section", chan, None),
        P("section", chan),
        P("section", chan, None),
        P(chan),
        P(chan, "dp", None, None),
    )
    out_specs = (
        P(chan, "dp", None, None),
        P("dp", "section", None, chan),
        P("section", None, chan),
        P("section", chan, None),
        P("section", chan),
        P("section", chan, None),
        P(chan),
    )
    return jax.shard_map(local, mesh=fine, in_specs=in_specs, out_specs=out_specs, check_vma=False)
```
